128 devices in a mesh: tensor: 2 (over core), req: 16 (over x, z), seq: 4 (over y).
Axes of the slice: x: 4, y: 4, z: 4, core: 2. Of those that a mesh axis runs over, the one named last changes fastest.
Arguments:
- incoming_activations: bfloat16 [32, 1024, 4096], P('req', 'seq'), may hold values from -6 to 6
- standardize_scaling: float32 [4096], replicated, may hold values from 0.1 to 1.9
- lagged_blending_weights: float32 [4, 4096], replicated, may hold values from 0 to 1
- learner_line_permutation: int32 [4096], replicated, may hold values from 0 to 4095, each once
- learner_acceptor_lookup_slices: float32 [3, 4096, 2048], P(None, ('req', 'seq'), 'tensor'), may hold values from -0.09375 to 0.09375
- learner_projection_slices: float32 [2048, 4096], P('tensor', ('req', 'seq')), may hold values from -0.125 to 0.125
- fading_left_matrix: bfloat16 [4096, 128], replicated, may hold values from -0.09375 to 0.09375
- fading_right_matrix: bfloat16 [128, 2048], P(None, 'tensor'), may hold values from -0.5 to 0.5
- feature_fading_speed: float32 [2048], P('tensor'), may hold values from 0.0002 to 0.08
- self_reward: float32 [2048], P('tensor'), may hold values from -3 to 3
- cluster_scaling_vector: float32 [2048], P('tensor'), may hold values from 0.1 to 1.9
- prompt_extents: int32 [32], P('req'), may hold values from 128 to 1024, as said below
Outputs:
- hidden_out: bfloat16 [32, 1024, 4096], P('req', 'seq', 'tensor')
- stretch_states: float32 [32, 4, 32, 4096], P('req', 'seq', 'tensor')
The draws below stay inside these ranges and needn't reach their ends.
Inputs may be any that keep to these rules, and one draw needn't show every extreme that they name: `prompt_extents`: it counts the valid tokens of each prompt from its start; prompt 0 is always full. learner_line_permutation names each of the 4096 input rows once.
All inputs are finite; a program needn't handle non-finite values.
Results may differ from the reference program's by a relative error of at most 0.013.
Values may be sent and summed in bfloat16 or wider, within the bound.
A program may use at most 192 MiB of HBM per device.

```python
import math
import jax
import jax.numpy as jnp
from jax import lax

MODEL_WIDTH = 4096
ATTEND_DIM = 64
MIDDLE_COUNT = 32
DECAY_INNER = 128
CH = 256
LEN = 1024
REQS = 32
STRETCHES = 4
ATTEND_FEATURES = 2048
N_TENSOR = 2


def draw_prompt_extents(key, part):
    drawn = jax.random.randint(key, (REQS,), LEN // 8, LEN + 1)
    return drawn.at[0].set(LEN).astype(jnp.int32)


def block_scale(stream_key, dims, split, low, largest):
    level, own = 1.0, jax.random.fold_in(stream_key, 6)
    for position, parts in split:
        draws = jnp.exp(jax.random.uniform(jax.random.fold_in(own, position), (parts,), jnp.float32, low / len(split), largest / len(split)))
        level = level * jnp.repeat(draws, dims[position] // parts).reshape([-1 if axis == position else 1 for axis in range(len(dims))])
    return level


def bell_draw(rng, shape, deviation, most, cuts=(), kind=jnp.bfloat16):
    entries = jax.random.normal(rng, shape, jnp.float32) * deviation
    if len(cuts) > 0:
        entries = block_scale(rng, shape, cuts, -0.22, 0.18) * entries
    return jnp.clip(entries, min=-most, max=most).astype(kind)


def setup_inputs(seed: int = 0) -> dict:
    key_list = jax.random.split(jax.random.key(seed), 13)
    return {
        "incoming_activations": bell_draw(key_list[0], (REQS, LEN, MODEL_WIDTH), 1.0, 6.0, ((0, 16), (1, 4))),
        "standardize_scaling": jnp.clip(1.0 + 0.18 * jax.random.normal(key_list[1], (MODEL_WIDTH,), jnp.float32), 0.1, 1.9),
        "lagged_blending_weights": jnp.clip(jax.random.uniform(key_list[2], (4, MODEL_WIDTH), jnp.float32, 0.0, 1.0), 0.0, 1.0),
        "learner_line_permutation": jax.random.permutation(key_list[3], MODEL_WIDTH).astype(jnp.int32),
        "learner_acceptor_lookup_slices": bell_draw(key_list[4], (3, MODEL_WIDTH, ATTEND_FEATURES), MODEL_WIDTH ** -0.5, 0.09375, ((1, 64), (2, 2)), jnp.float32),
        "learner_projection_slices": bell_draw(key_list[5], (ATTEND_FEATURES, MODEL_WIDTH), ATTEND_FEATURES ** -0.5, 0.125, ((0, 2), (1, 64)), jnp.float32),
        "fading_left_matrix": bell_draw(key_list[6], (MODEL_WIDTH, DECAY_INNER), MODEL_WIDTH ** -0.5, 0.09375),
        "fading_right_matrix": bell_draw(key_list[7], (DECAY_INNER, ATTEND_FEATURES), DECAY_INNER ** -0.5, 0.5, ((1, 2),)),
        "feature_fading_speed": jnp.clip(jnp.exp(math.log(0.08) - 5.9914646 * jax.random.uniform(key_list[8], (ATTEND_FEATURES,), jnp.float32) ** block_scale(key_list[8], (ATTEND_FEATURES,), ((0, 2),), -0.2, 0.2)), 0.0002, 0.08),
        "self_reward": bell_draw(key_list[9], (ATTEND_FEATURES,), 1.0, 3.0, ((0, 2),), jnp.float32),
        "cluster_scaling_vector": jnp.clip(1.0 + 0.18 * jax.random.normal(key_list[10], (ATTEND_FEATURES,), jnp.float32), 0.1, 1.9),
        "prompt_extents": draw_prompt_extents(jax.random.fold_in(key_list[12], 71), 0),
    }


eps = 1e-05

def layer_norm(values, gain):
    mean = lax.optimization_barrier(jnp.mean(values, axis=-1, keepdims=True))
    centred = values - mean
    spread = lax.optimization_barrier(jnp.mean(centred * centred, axis=-1, keepdims=True))
    return centred * lax.rsqrt(spread + eps) * gain

def reference(incoming_activations, standardize_scaling, lagged_blending_weights, learner_line_permutation, learner_acceptor_lookup_slices, learner_projection_slices, fading_left_matrix, fading_right_matrix, feature_fading_speed, self_reward, cluster_scaling_vector, prompt_extents):
    current = layer_norm(incoming_activations.astype(jnp.float32), standardize_scaling)
    previous = jnp.concatenate([jnp.zeros_like(current[:, :1]), current[:, :-1]], axis=1)
    delta = previous - current
    shift_mixed = [(current + delta * lagged_blending_weights[j]).astype(jnp.bfloat16) for j in range(4)]
    valid_mask = (jnp.arange(LEN, dtype=jnp.int32)[None, :] < prompt_extents[:, None]).astype(jnp.float32)[..., None]
    stored = []
    for j in range(3):
        weight = learner_acceptor_lookup_slices[j].astype(jnp.bfloat16)
        product = jnp.dot(shift_mixed[j][..., learner_line_permutation], weight, preferred_element_type=jnp.float32)
        stored.append(lax.optimization_barrier(product.astype(jnp.bfloat16)).astype(jnp.float32))
    receptance = stored[0]
    keys = stored[1] * valid_mask
    values = stored[2]
    decay_lowrank = jnp.tanh(jnp.dot(shift_mixed[3], fading_left_matrix, preferred_element_type=jnp.float32)).astype(jnp.bfloat16)
    decay_logarithm = -feature_fading_speed * jnp.exp(jnp.dot(decay_lowrank, fading_right_matrix, preferred_element_type=jnp.float32)) * valid_mask

    def heads_first(array):
        return jnp.transpose(array.reshape(REQS, LEN, MIDDLE_COUNT, ATTEND_DIM), (1, 0, 2, 3))
    seq_r = heads_first(receptance)
    seq_k = heads_first(keys)
    seq_v = heads_first(values)
    seq_w = heads_first(decay_logarithm)
    attender_reward = self_reward.reshape(MIDDLE_COUNT, ATTEND_DIM)

    def advance(carried_memory, items):
        acceptor_moment, k_t, v_t, w_t = items
        tensor_dyad = k_t[..., :, None] * v_t[..., None, :]
        sublevel_result = jnp.einsum('zhb,zhbs->zhs', acceptor_moment, carried_memory + attender_reward[None, :, :, None] * tensor_dyad, precision=lax.Precision.HIGHEST)
        carried_memory = jnp.exp(w_t)[..., None] * carried_memory + tensor_dyad
        return (carried_memory, sublevel_result)
    carried_memory = jnp.zeros((REQS, MIDDLE_COUNT, ATTEND_DIM, ATTEND_DIM), jnp.float32)
    pieces = []
    saved = []
    for block in range(STRETCHES):
        lo = block * CH
        carried_memory, sublevel_result = lax.scan(advance, carried_memory, (seq_r[lo:lo + CH], seq_k[lo:lo + CH], seq_v[lo:lo + CH], seq_w[lo:lo + CH]))
        pieces.append(sublevel_result)
        saved.append(carried_memory.reshape(REQS, MIDDLE_COUNT, ATTEND_DIM * ATTEND_DIM))
    y_all = jnp.transpose(jnp.concatenate(pieces, axis=0), (1, 0, 2, 3))
    stretch_states = jnp.stack(saved, axis=1)
    mean = lax.optimization_barrier(jnp.mean(y_all, axis=-1, keepdims=True))
    centred = y_all - mean
    spread = lax.optimization_barrier(jnp.mean(centred * centred, axis=-1, keepdims=True))
    normed = centred * lax.rsqrt(spread + eps) * cluster_scaling_vector.reshape(MIDDLE_COUNT, ATTEND_DIM)
    normed = (normed.reshape(REQS, LEN, ATTEND_FEATURES) * valid_mask).astype(jnp.bfloat16)
    out_weight = learner_projection_slices.astype(jnp.bfloat16)
    group = ATTEND_FEATURES // N_TENSOR
    total = jnp.zeros((REQS, LEN, MODEL_WIDTH), jnp.float32)
    for g in range(N_TENSOR):
        part = jnp.dot(normed[..., g * group:(g + 1) * group], out_weight[g * group:(g + 1) * group], preferred_element_type=jnp.float32)
        total = total + lax.optimization_barrier(part.astype(jnp.bfloat16)).astype(jnp.float32)
    hidden_out = (incoming_activations.astype(jnp.float32) + total).astype(jnp.bfloat16)
    return (hidden_out, stretch_states)
```

```python
import functools

import jax
import jax.numpy as jnp
from jax import lax
from jax.experimental import pallas as pl
from jax.experimental.pallas import tpu as pltpu
from jax.sharding import PartitionSpec as P

ATTEND_DIM = 64
PAIR = 128
CHUNK = 128
COLS = 256
SAFE = -60.0
eps = 1e-05
f32 = jnp.float32
bf16 = jnp.bfloat16
HIGHEST = lax.Precision.HIGHEST
CONTRACT_ROWS = (((0,), (0,)), ((), ()))
CONTRACT_LANES = (((1,), (1,)), ((), ()))


def from_behind(value, axis, by):
    peers = lax.axis_size(axis)
    pairs = [(i, i + by) for i in range(peers) if 0 <= i + by < peers]
    return lax.ppermute(value, axis, pairs)


def split_two(value):
    high = value.astype(bf16)
    low = (value - high.astype(f32)).astype(bf16)
    return high, low


def dot32(a, b, dims=(((1,), (0,)), ((), ()))):
    return lax.dot_general(a, b, dims, preferred_element_type=f32)


def mix_kernel(
    x_ref, tail_ref, perm_ref, gain_ref, blend_ref, left_ref, mr_ref, mk_ref, mv_ref, lora_ref,
    stack, chosen, stats, low_rank,
):
    rows, width = x_ref.shape
    span = rows // tail_ref.shape[0]
    step = pl.program_id(0)

    @pl.when(step == 0)
    def _():
        stack[:rows, :] = x_ref[...]
        table = jnp.concatenate([gain_ref[...], blend_ref[0:3, :]], axis=0)
        first = table.astype(bf16)
        rest = table - first.astype(f32)
        second = rest.astype(bf16)
        third = (rest - second.astype(f32)).astype(bf16)
        pad = jnp.zeros((2, width), bf16)
        stack[rows:, :] = jnp.concatenate([tail_ref[...], first, second, third, pad], axis=0)
        low_rank[...] = jnp.zeros_like(low_rank)

        def row_stats(i, _):
            at = pl.ds(pl.multiple_of(i * 16, 16), 16)
            part = stack[at, :].astype(f32)
            mean = jnp.mean(part, axis=-1, keepdims=True)
            centred = part - mean
            spread = jnp.mean(centred * centred, axis=-1, keepdims=True)
            stats[0, at, :] = jnp.broadcast_to(mean, (16, PAIR))
            stats[1, at, :] = jnp.broadcast_to(lax.rsqrt(spread + eps), (16, PAIR))
            return 0

        lax.fori_loop(0, stack.shape[0] // 16, row_stats, 0)

    mean, scale = stats[0, :, 0:1], stats[1, :, 0:1]
    row = lax.broadcasted_iota(jnp.int32, (rows, 1), 0)

    def shifted(values, gain):
        normal = (values - mean[: values.shape[0]]) * scale[: values.shape[0]] * gain
        current = normal[:rows]
        previous = pltpu.roll(current, 1, axis=0)
        for b in range(rows // span):
            previous = jnp.where(row == b * span, normal[rows + b : rows + b + 1], previous)
        return current, previous - current

    names = perm_ref[...]

    def one_hot(i, _):
        base = pl.multiple_of(i * COLS, COLS)
        feature = lax.broadcasted_iota(jnp.int32, (COLS, COLS), 0) + base
        chosen[pl.ds(base, COLS), :] = (feature == names).astype(f32).astype(bf16)
        return 0

    lax.fori_loop(0, width // COLS, one_hot, 0)
    picked = dot32(stack[...], chosen[...])
    table = picked[rows + 2 : rows + 6] + picked[rows + 6 : rows + 10] + picked[rows + 10 : rows + 14]
    current, delta = shifted(picked, table[0:1])
    mr_ref[...] = (current + delta * table[1:2]).astype(bf16)
    mk_ref[...] = (current + delta * table[2:3]).astype(bf16)
    mv_ref[...] = (current + delta * table[3:4]).astype(bf16)

    here = pl.ds(pl.multiple_of(step * COLS, COLS), COLS)
    current, delta = shifted(stack[:, here].astype(f32), gain_ref[:, here])
    mixed = (current + delta * blend_ref[3:4, here]).astype(bf16)
    low_rank[...] += dot32(mixed, left_ref[...])

    @pl.when(step == pl.num_programs(0) - 1)
    def _():
        lora_ref[...] = jnp.tanh(low_rank[...]).astype(bf16)


def mix(x, tail, perm, gain, blend, left):
    rows, width = x.shape
    whole = lambda shape: pl.BlockSpec(shape, lambda i: (0,) * len(shape))
    column = pl.BlockSpec((rows, COLS), lambda i: (0, i))
    out = jax.ShapeDtypeStruct((rows, width), bf16)
    return pl.pallas_call(
        mix_kernel,
        grid=(width // COLS,),
        in_specs=[
            whole((rows, width)),
            whole(tail.shape),
            pl.BlockSpec((1, COLS), lambda i: (0, i)),
            whole((1, width)),
            whole((4, width)),
            pl.BlockSpec((COLS, left.shape[1]), lambda i: (i, 0)),
        ],
        out_specs=[column, column, column, whole((rows, left.shape[1]))],
        out_shape=[out, out, out, jax.ShapeDtypeStruct((rows, left.shape[1]), bf16)],
        scratch_shapes=[
            pltpu.VMEM((rows + 16, width), bf16),
            pltpu.VMEM((width, COLS), bf16),
            pltpu.VMEM((2, rows + 16, PAIR), f32),
            pltpu.VMEM((rows, left.shape[1]), f32),
        ],
        compiler_params=pltpu.CompilerParams(vmem_limit_bytes=48 << 20),
        cost_estimate=pl.CostEstimate(
            flops=2 * rows * width * width, bytes_accessed=16 * rows * width, transcendentals=0
        ),
        name="mix",
    )(x, tail, perm, gain, blend, left)


def earlier(size):
    t = lax.broadcasted_iota(jnp.int32, (size, size), 0)
    s = lax.broadcasted_iota(jnp.int32, (size, size), 1)
    return t > s


def same_head():
    c = lax.broadcasted_iota(jnp.int32, (PAIR, PAIR), 0) // ATTEND_DIM
    v = lax.broadcasted_iota(jnp.int32, (PAIR, PAIR), 1) // ATTEND_DIM
    return c == v


def sum_before(decays):
    ones = earlier(decays.shape[0]).astype(f32).astype(bf16)
    high, low = split_two(decays)
    return dot32(ones, high) + dot32(ones, low)


def sum_after(decays):
    ones = earlier(decays.shape[0]).astype(f32).astype(bf16)
    high, low = split_two(decays)
    return dot32(ones, high, CONTRACT_ROWS) + dot32(ones, low, CONTRACT_ROWS)


def column_total(decays):
    high, low = split_two(decays)
    ones = jnp.ones((decays.shape[0], PAIR), bf16)
    return dot32(high, ones, CONTRACT_ROWS) + dot32(low, ones, CONTRACT_ROWS)


def state_kernel(span, valid_ref, lora_ref, right_ref, speed_ref, k_ref, v_ref, w_ref, l_ref, t_ref):
    rows = k_ref.shape[0]
    valid = valid_ref[:, 0:1]
    log_decay = -speed_ref[...] * jnp.exp(dot32(lora_ref[...], right_ref[...])) * valid
    w_ref[...] = log_decay
    keep = same_head()
    for b in range(rows // span):
        at = slice(b * span, (b + 1) * span)
        part = log_decay[at]
        left_over = jnp.exp(sum_after(part))
        key = (k_ref[at].astype(f32) * valid[at] * left_over).astype(bf16)
        state = dot32(key, v_ref[at], CONTRACT_ROWS)
        l_ref[b, 0] = jnp.where(keep, state, 0.0).astype(l_ref.dtype)
        t_ref[b, 0] = column_total(part)


def local_states(valid, lora, right, speed, k, v, span):
    rows, width = k.shape
    pairs, reqs = width // PAIR, rows // span
    column = pl.BlockSpec((rows, PAIR), lambda i: (0, i))
    whole = lambda shape: pl.BlockSpec(shape, lambda i: (0,) * len(shape))
    piece = pl.BlockSpec((reqs, 1, PAIR, PAIR), lambda i: (0, i, 0, 0))
    return pl.pallas_call(
        functools.partial(state_kernel, span),
        grid=(pairs,),
        in_specs=[
            whole(valid.shape), whole(lora.shape),
            pl.BlockSpec((right.shape[0], PAIR), lambda i: (0, i)),
            pl.BlockSpec((1, PAIR), lambda i: (0, i)),
            column, column,
        ],
        out_specs=[column, piece, piece],
        out_shape=[
            jax.ShapeDtypeStruct((rows, width), f32),
            jax.ShapeDtypeStruct((reqs, pairs, PAIR, PAIR), bf16),
            jax.ShapeDtypeStruct((reqs, pairs, PAIR, PAIR), f32),
        ],
        compiler_params=pltpu.CompilerParams(vmem_limit_bytes=32 << 20),
        cost_estimate=pl.CostEstimate(flops=10**9, bytes_accessed=8 << 20, transcendentals=10**6),
        name="local_states",
    )(valid, lora, right, speed, k, v)


def within_chunk_stepwise(r, k, v, w):
    rows = lax.broadcasted_iota(jnp.int32, (CHUNK, 1), 0)
    ones = jnp.ones((CHUNK, PAIR), f32)
    keep = same_head()

    def token(t, carried):
        state, out = carried
        mine = rows == t
        dot = functools.partial(lax.dot_general, precision=HIGHEST, preferred_element_type=f32)
        out = out + dot(jnp.where(mine, r, 0.0), state, (((1,), (0,)), ((), ())))
        fade = jnp.exp(dot(jnp.where(mine, w, 0.0), ones, CONTRACT_ROWS))
        dyad = jnp.where(keep, dot(jnp.where(mine, k, 0.0), v, CONTRACT_ROWS), 0.0)
        return fade * state + dyad, out

    zero = jnp.zeros((PAIR, PAIR), f32)
    return lax.fori_loop(0, CHUNK, token, (zero, jnp.zeros((CHUNK, PAIR), f32)))[1]


def read_kernel(
    span, valid_ref, r_ref, k_ref, v_ref, w_ref, in_ref, l_ref, t_ref, reward_ref, scale_ref,
    out_ref, state_ref, inner,
):
    rows = k_ref.shape[0]
    keep = same_head()
    average = jnp.where(keep, 1.0, 0.0).astype(bf16)
    first_head = lax.broadcasted_iota(jnp.int32, (1, PAIR), 1) < ATTEND_DIM
    strict = earlier(CHUNK)
    strict = jnp.concatenate([strict, strict], axis=1)
    for b in range(rows // span):
        state = in_ref[b, 0]
        final = jnp.exp(t_ref[b, 0]) * state + l_ref[b, 0].astype(f32)
        state_ref[b, 0, 0] = final[:ATTEND_DIM, :ATTEND_DIM]
        state_ref[b, 0, 1] = final[ATTEND_DIM:, ATTEND_DIM:]
        for c in range(span // CHUNK):
            at = slice(b * span + c * CHUNK, b * span + (c + 1) * CHUNK)
            valid = valid_ref[at, 0:1]
            r, v = r_ref[at].astype(f32), v_ref[at]
            k = k_ref[at].astype(f32) * valid
            w = w_ref[at]
            before = sum_before(w)
            cum = before + w
            mid, last = before[CHUNK // 2 : CHUNK // 2 + 1], cum[CHUNK - 1 :]
            gentle = jnp.min(jnp.minimum(mid, last - mid)) > SAFE

            @pl.when(gentle)
            def _():
                query = (r * jnp.exp(before - mid)).astype(bf16)
                key = k * jnp.exp(mid - cum)
                keys = jnp.concatenate(
                    [jnp.where(first_head, key, 0.0), jnp.where(first_head, 0.0, key)], axis=0
                ).astype(bf16)
                scores = jnp.where(strict, dot32(query, keys, CONTRACT_LANES), 0.0).astype(bf16)
                value = v.astype(f32)
                values = jnp.concatenate(
                    [jnp.where(first_head, value, 0.0), jnp.where(first_head, 0.0, value)], axis=0
                ).astype(bf16)
                inner[...] = dot32(scores, values)

            @pl.when(jnp.logical_not(gentle))
            def _():
                inner[...] = within_chunk_stepwise(r, k, v.astype(f32), w)

            high, low = split_two(r * reward_ref[...] * k)
            own = (dot32(high, average) + dot32(low, average)) * v.astype(f32)
            y = inner[...] + own + dot32((r * jnp.exp(before)).astype(bf16), state.astype(bf16))
            if c + 1 < span // CHUNK:
                left_over = (k * jnp.exp(sum_after(w))).astype(bf16)
                grown = dot32(left_over, v, CONTRACT_ROWS)
                state = jnp.exp(column_total(w)) * state + jnp.where(keep, grown, 0.0)
            high, low = split_two(y)
            centred = y - (dot32(high, average) + dot32(low, average)) * (1.0 / ATTEND_DIM)
            high, low = split_two(centred * centred)
            spread = (dot32(high, average) + dot32(low, average)) * (1.0 / ATTEND_DIM)
            normed = centred * lax.rsqrt(spread + eps) * scale_ref[...] * valid
            out_ref[at] = normed.astype(bf16)


def read_states(valid, r, k, v, w, incoming, local_state, totals, reward, scale, span):
    rows, width = k.shape
    pairs, reqs = width // PAIR, rows // span
    column = pl.BlockSpec((rows, PAIR), lambda i: (0, i))
    line = pl.BlockSpec((1, PAIR), lambda i: (0, i))
    piece = pl.BlockSpec((reqs, 1, PAIR, PAIR), lambda i: (0, i, 0, 0))
    heads = pl.BlockSpec((reqs, 1, 2, ATTEND_DIM, ATTEND_DIM), lambda i: (0, i, 0, 0, 0))
    return pl.pallas_call(
        functools.partial(read_kernel, span),
        grid=(pairs,),
        in_specs=[
            pl.BlockSpec(valid.shape, lambda i: (0, 0)),
            column, column, column, column, piece, piece, piece, line, line,
        ],
        out_specs=[column, heads],
        out_shape=[
            jax.ShapeDtypeStruct((rows, width), bf16),
            jax.ShapeDtypeStruct((reqs, pairs, 2, ATTEND_DIM, ATTEND_DIM), f32),
        ],
        scratch_shapes=[pltpu.VMEM((CHUNK, PAIR), f32)],
        compiler_params=pltpu.CompilerParams(vmem_limit_bytes=32 << 20),
        cost_estimate=pl.CostEstimate(flops=2 * 10**9, bytes_accessed=8 << 20, transcendentals=10**6),
        name="read_states",
    )(valid, r, k, v, w, incoming, local_state, totals, reward, scale)


def local(
    incoming_activations,
    standardize_scaling,
    lagged_blending_weights,
    learner_line_permutation,
    learner_acceptor_lookup_slices,
    learner_projection_slices,
    fading_left_matrix,
    fading_right_matrix,
    feature_fading_speed,
    self_reward,
    cluster_scaling_vector,
    prompt_extents,
):
    reqs, span, width = incoming_activations.shape
    rows = reqs * span
    local_width = feature_fading_speed.shape[0]
    pairs = local_width // PAIR
    x = incoming_activations.reshape(rows, width)
    weights = learner_acceptor_lookup_slices.astype(bf16)
    gather = functools.partial(lax.all_gather, axis_name=("req", "seq"), tiled=True)
    weight_k = gather(weights[1], axis=0)
    weight_v = gather(weights[2], axis=0)
    weight_r = gather(weights[0], axis=0)
    weight_out = gather(learner_projection_slices.T.astype(bf16), axis=0)
    tail = from_behind(incoming_activations[:, span - 1, :], "seq", 1)
    positions = lax.axis_index("seq") * span + jnp.arange(span, dtype=jnp.int32)
    valid = (positions[None, :] < prompt_extents[:, None]).astype(f32).reshape(rows, 1)
    valid = jnp.broadcast_to(valid, (rows, PAIR))
    mixed_r, mixed_k, mixed_v, lora = mix(
        x, tail, learner_line_permutation[None], standardize_scaling[None],
        lagged_blending_weights, fading_left_matrix,
    )
    k = dot32(mixed_k, weight_k).astype(bf16)
    v = dot32(mixed_v, weight_v).astype(bf16)
    decays, states, totals = local_states(
        valid, lora, fading_right_matrix, feature_fading_speed[None], k, v, span
    )
    incoming = jnp.zeros(states.shape, f32)
    sent = jnp.zeros_like(totals)
    for by in range(1, lax.axis_size("seq")):
        far_state = from_behind(states, "seq", by).astype(f32)
        incoming = incoming + jnp.exp(sent) * far_state
        if by + 1 < lax.axis_size("seq"):
            far_total = from_behind(totals[..., 0], "seq", by)
            sent = sent + far_total[..., None]
    r = dot32(mixed_r, weight_r).astype(bf16)
    normed, final = read_states(
        valid, r, k, v, decays, incoming, states, totals,
        self_reward[None], cluster_scaling_vector[None], span,
    )
    stretch_states = final.reshape(reqs, 1, local_width // ATTEND_DIM, ATTEND_DIM * ATTEND_DIM)
    terms = dot32(normed, weight_out, CONTRACT_LANES)
    summed = lax.psum_scatter(
        terms.astype(bf16), "tensor", scatter_dimension=1, tiled=True
    ).astype(f32)
    share = width // lax.axis_size("tensor")
    residual = lax.dynamic_slice_in_dim(x, lax.axis_index("tensor") * share, share, 1)
    hidden_out = (residual.astype(f32) + summed).astype(bf16).reshape(reqs, span, share)
    return (hidden_out, stretch_states)


def solution(mesh):
    in_specs = (
        P("req", "seq", None),
        P(),
        P(),
        P(),
        P(None, ("req", "seq"), "tensor"),
        P("tensor", ("req", "seq")),
        P(),
        P(None, "tensor"),
        P("tensor"),
        P("tensor"),
        P("tensor"),
        P("req"),
    )
    out_specs = (P("req", "seq", "tensor"), P("req", "seq", "tensor", None))
    return jax.shard_map(local, mesh=mesh, in_specs=in_specs, out_specs=out_specs, check_vma=False)
```

```python
import functools

import jax
import jax.numpy as jnp
from jax import lax
from jax.experimental import pallas as pl
from jax.experimental.pallas import tpu as pltpu
from jax.sharding import PartitionSpec as P

ATTEND_DIM = 64
PAIR = 128
CHUNK = 128
SAFE = -60.0
eps = 1e-05
f32 = jnp.float32
bf16 = jnp.bfloat16
HIGHEST = lax.Precision.HIGHEST
CONTRACT_ROWS = (((0,), (0,)), ((), ()))
CONTRACT_LANES = (((1,), (1,)), ((), ()))


def from_behind(value, axis, by):
    peers = lax.axis_size(axis)
    pairs = [(i, i + by) for i in range(peers) if 0 <= i + by < peers]
    return lax.ppermute(value, axis, pairs)


def split_two(value):
    high = value.astype(bf16)
    low = (value - high.astype(f32)).astype(bf16)
    return high, low


def dot32(a, b, dims=(((1,), (0,)), ((), ()))):
    return lax.dot_general(a, b, dims, preferred_element_type=f32)


MESH = pl.DeviceIdType.MESH
ORDERS = (("x", "y", "z"), ("y", "z", "x"), ("z", "x", "y"))
PLACES = (("z", "y", "x"), ("x", "y", "z"), ("y", "x", "z"))
SIDE = 4
STEP = 512


def position():
    req = lax.axis_index("req")
    return {"x": req // SIDE, "z": req % SIDE, "y": lax.axis_index("seq")}


def moved(at, axis, by):
    return {**at, axis: (at[axis] + by + SIDE) % SIDE}


def device(at):
    return (lax.axis_index("tensor"), at["x"] * SIDE + at["z"], at["y"])


def greet_neighbours(at):
    barrier = pltpu.get_barrier_semaphore()
    for axis in "xyz":
        for by in (1, -1):
            pl.semaphore_signal(
                barrier, inc=1, device_id=device(moved(at, axis, by)), device_id_type=MESH
            )
    pl.semaphore_wait(barrier, 6)


class Ring:
    def __init__(self, slots, order, places, send, recv, parts):
        self.slots, self.order, self.places = slots, order, places
        self.send, self.recv, self.parts = send, recv, parts
        self.at = position()

    def block(self, phase, where, part):
        index = []
        for axis in self.places:
            turn = self.order.index(axis)
            index.append(slice(None) if turn < phase else where if turn == phase else self.at[axis])
        return self.slots.at[(*index, *part)]

    def copy(self, phase, kind, right):
        axis = self.order[phase]
        to = moved(self.at, axis, 1 if right else -1)
        if kind == 0:
            ref = self.block(phase, self.at[axis], ())
        else:
            source = moved(self.at, axis, -1 if right else 1)[axis]
            ref = self.block(phase, source, (self.parts[0 if right else 1],))
        slot = 2 * kind + (0 if right else 1)
        return pltpu.make_async_remote_copy(
            ref, ref, self.send.at[phase, slot], self.recv.at[phase, slot],
            device_id=device(to), device_id_type=MESH,
        )

    def start(self, phase, kind):
        for right in (True, False):
            self.copy(phase, kind, right).start()

    def arrived(self, phase, kind):
        for right in (True, False):
            self.copy(phase, kind, right).wait_recv()

    def finish(self):
        for phase in range(3):
            for kind in range(2):
                for right in (True, False):
                    self.copy(phase, kind, right).wait_send()


def project_kernel(
    x_ref, last_ref, perm_ref, gain_ref, blend_ref, left_ref, w_ref, out_ref, lora_ref,
    slots, stack, mixed, chosen, picked, total, stats, low_rank, tail, load_sem, tail_sem, send, recv,
):
    rows, width = x_ref.shape
    reqs = last_ref.shape[0]
    span = rows // reqs
    at = position()
    half = w_ref.shape[1] // 2
    parts = (slice(0, half), slice(half, 2 * half))
    rings = [
        Ring(slots.at[m], ORDERS[m], PLACES[m], send.at[m], recv.at[m], parts) for m in range(3)
    ]
    load = pltpu.make_async_copy(x_ref, stack.at[pl.ds(0, rows)], load_sem)
    load.start()
    for m in range(3):
        slots[(m, *(at[axis] for axis in PLACES[m]))] = w_ref[m].astype(bf16)
    greet_neighbours(at)
    hand_on = pltpu.make_async_remote_copy(
        last_ref, tail, tail_sem.at[0], tail_sem.at[1],
        device_id=device(moved(at, "y", 1)), device_id_type=MESH,
    )
    hand_on.start()
    for ring in rings:
        ring.start(0, 0)

    table = jnp.concatenate([gain_ref[...], blend_ref[0:3, :]], axis=0)
    first = table.astype(bf16)
    rest = table - first.astype(f32)
    second = rest.astype(bf16)
    third = (rest - second.astype(f32)).astype(bf16)
    hand_on.wait_recv()
    before = jnp.where(at["y"] > 0, tail[...].astype(f32), 0.0).astype(bf16)
    pad = jnp.zeros((16 - reqs - 12, width), bf16)
    stack[rows:, :] = jnp.concatenate([before, first, second, third, pad], axis=0)
    low_rank[...] = jnp.zeros_like(low_rank)
    load.wait()

    def row_stats(i, _):
        here = pl.ds(pl.multiple_of(i * 16, 16), 16)
        part = stack[here, :].astype(f32)
        mean = jnp.mean(part, axis=-1, keepdims=True)
        centred = part - mean
        spread = jnp.mean(centred * centred, axis=-1, keepdims=True)
        stats[0, here, :] = jnp.broadcast_to(mean, (16, PAIR))
        stats[1, here, :] = jnp.broadcast_to(lax.rsqrt(spread + eps), (16, PAIR))
        return 0

    lax.fori_loop(0, stack.shape[0] // 16, row_stats, 0)

    def shifted(values, gain):
        mean, scale = stats[0, :, 0:1], stats[1, :, 0:1]
        row = lax.broadcasted_iota(jnp.int32, (rows, 1), 0)
        normal = (values - mean) * scale * gain
        current = normal[:rows]
        previous = pltpu.roll(current, 1, axis=0)
        for b in range(reqs):
            previous = jnp.where(row == b * span, normal[rows + b : rows + b + 1], previous)
        return current, previous - current

    piece = STEP // 2
    depth = chosen.shape[0]

    def mix_step(step, _):
        here = pl.ds(pl.multiple_of(step * STEP, STEP), STEP)
        names = perm_ref[:, here]
        picked[...] = jnp.zeros_like(picked)

        def pick(d, _):
            def one_hot(i, _):
                base = pl.multiple_of(i * 128, 128)
                feature = lax.broadcasted_iota(jnp.int32, (128, STEP), 0) + (base + d * depth)
                chosen[pl.ds(base, 128), :] = (feature == names).astype(f32).astype(bf16)
                return 0

            lax.fori_loop(0, depth // 128, one_hot, 0)
            source = stack[:, pl.ds(pl.multiple_of(d * depth, depth), depth)]
            picked[...] += dot32(source, chosen[...])
            return 0

        lax.fori_loop(0, width // depth, pick, 0)
        y, x0 = step // 2, (step % 2) * 2
        for i in range(2):
            values = picked[:, i * piece : (i + 1) * piece]
            own = values[rows + reqs :]
            own = own[0:4] + own[4:8] + own[8:12]
            current, delta = shifted(values, own[0:1])
            blended = [(current + delta * own[1 + j : 2 + j]).astype(bf16) for j in range(3)]
            picked[:rows, i * piece : (i + 1) * piece] = blended[0].astype(f32)
            mixed[1, x0 + i, :, pl.ds(pl.multiple_of(y * piece, piece), piece)] = blended[1]
            mixed[2, y, :, pl.ds(pl.multiple_of((x0 + i) * piece, piece), piece)] = blended[2]
        columns = pl.ds(pl.multiple_of(step * 128, 128), 128)
        for z in range(SIDE):
            pair = [picked[:rows, i * piece + z * 64 : i * piece + (z + 1) * 64] for i in range(2)]
            mixed[0, z, :, columns] = jnp.concatenate(pair, axis=1).astype(bf16)

        current, delta = shifted(stack[:, here].astype(f32), gain_ref[:, here])
        low_rank[...] += dot32(
            (current + delta * blend_ref[3:4, here]).astype(bf16),
            left_ref[pl.ds(pl.multiple_of(step * STEP, STEP), STEP), :],
        )

        @pl.when(step == 0)
        def _():
            for ring in rings:
                ring.arrived(0, 0)
                ring.start(0, 1)

        @pl.when(step == 1)
        def _():
            for ring in rings:
                ring.arrived(0, 1)
                ring.start(1, 0)

        @pl.when(step == 3)
        def _():
            for ring in rings:
                ring.arrived(1, 0)
                ring.start(1, 1)

        @pl.when(step == 4)
        def _():
            for ring in rings:
                ring.arrived(1, 1)
                ring.start(2, 0)

        return 0

    lax.fori_loop(0, width // STEP, mix_step, 0)
    lora_ref[...] = jnp.tanh(low_rank[...]).astype(bf16)

    def products(offset, fresh):
        def tile(i, _):
            m, n = i // 4, i % 4
            own = jnp.where(m == 0, at["z"], jnp.where(m == 1, at["x"], at["y"]))
            plane = (own + offset) % SIDE
            here = pl.ds(pl.multiple_of(n * 256, 256), 256)
            weight = slots[m, plane, :, :, :, here].reshape(width // SIDE, 256)
            product = dot32(mixed[m, plane], weight)
            if fresh:
                total[m, :, here] = product
            elif offset == 2:
                out_ref[m, :, here] = (total[m, :, here] + product).astype(bf16)
            else:
                total[m, :, here] += product
            return 0

        lax.fori_loop(0, 12, tile, 0)

    products(0, True)
    for ring in rings:
        ring.arrived(2, 0)
        ring.start(2, 1)
    products(1, False)
    products(3, False)
    for ring in rings:
        ring.arrived(2, 1)
    products(2, False)
    hand_on.wait_send()
    for ring in rings:
        ring.finish()


def project(x, last, perm, gain, blend, left, weights):
    rows, width = x.shape
    inner, local_width = left.shape[1], weights.shape[2]
    vmem = pl.BlockSpec(memory_space=pltpu.VMEM)
    return pl.pallas_call(
        project_kernel,
        in_specs=[pl.BlockSpec(memory_space=pl.ANY)] + [vmem] * 6,
        out_specs=[vmem, vmem],
        out_shape=[
            jax.ShapeDtypeStruct((3, rows, local_width), bf16),
            jax.ShapeDtypeStruct((rows, inner), bf16),
        ],
        scratch_shapes=[
            pltpu.VMEM((3, SIDE, SIDE, SIDE, *weights.shape[1:]), bf16),
            pltpu.VMEM((rows + 16, width), bf16),
            pltpu.VMEM((3, SIDE, rows, width // SIDE), bf16),
            pltpu.VMEM((width // 2, STEP), bf16),
            pltpu.VMEM((rows + 16, STEP), f32),
            pltpu.VMEM((3, rows, local_width), f32),
            pltpu.VMEM((2, rows + 16, PAIR), f32),
            pltpu.VMEM((rows, inner), f32),
            pltpu.VMEM(last.shape, bf16),
            pltpu.SemaphoreType.DMA,
            pltpu.SemaphoreType.DMA((2,)),
            pltpu.SemaphoreType.DMA((3, 3, 4)),
            pltpu.SemaphoreType.DMA((3, 3, 4)),
        ],
        compiler_params=pltpu.CompilerParams(
            collective_id=0, has_side_effects=True, vmem_limit_bytes=61 << 20
        ),
        cost_estimate=pl.CostEstimate(
            flops=100 * 10**9, bytes_accessed=32 << 20, transcendentals=0
        ),
        name="project",
    )(x, last, perm, gain, blend, left, weights)


def earlier(size):
    t = lax.broadcasted_iota(jnp.int32, (size, size), 0)
    s = lax.broadcasted_iota(jnp.int32, (size, size), 1)
    return t > s


def same_head():
    c = lax.broadcasted_iota(jnp.int32, (PAIR, PAIR), 0) // ATTEND_DIM
    v = lax.broadcasted_iota(jnp.int32, (PAIR, PAIR), 1) // ATTEND_DIM
    return c == v


def sum_before(decays):
    ones = earlier(decays.shape[0]).astype(f32).astype(bf16)
    high, low = split_two(decays)
    return dot32(ones, high) + dot32(ones, low)


def sum_after(decays):
    ones = earlier(decays.shape[0]).astype(f32).astype(bf16)
    high, low = split_two(decays)
    return dot32(ones, high, CONTRACT_ROWS) + dot32(ones, low, CONTRACT_ROWS)


def column_total(decays):
    high, low = split_two(decays)
    ones = jnp.ones((decays.shape[0], PAIR), bf16)
    return dot32(high, ones, CONTRACT_ROWS) + dot32(low, ones, CONTRACT_ROWS)


def state_kernel(span, valid_ref, lora_ref, right_ref, speed_ref, k_ref, v_ref, w_ref, l_ref, t_ref):
    rows = k_ref.shape[0]
    valid = valid_ref[:, 0:1]
    log_decay = -speed_ref[...] * jnp.exp(dot32(lora_ref[...], right_ref[...])) * valid
    w_ref[...] = log_decay
    keep = same_head()
    for b in range(rows // span):
        at = slice(b * span, (b + 1) * span)
        part = log_decay[at]
        left_over = jnp.exp(sum_after(part))
        key = (k_ref[at].astype(f32) * valid[at] * left_over).astype(bf16)
        state = dot32(key, v_ref[at], CONTRACT_ROWS)
        l_ref[b, 0] = jnp.where(keep, state, 0.0).astype(l_ref.dtype)
        t_ref[b, 0] = column_total(part)


def local_states(valid, lora, right, speed, k, v, span):
    rows, width = k.shape
    pairs, reqs = width // PAIR, rows // span
    column = pl.BlockSpec((rows, PAIR), lambda i: (0, i))
    whole = lambda shape: pl.BlockSpec(shape, lambda i: (0,) * len(shape))
    piece = pl.BlockSpec((reqs, 1, PAIR, PAIR), lambda i: (0, i, 0, 0))
    return pl.pallas_call(
        functools.partial(state_kernel, span),
        grid=(pairs,),
        in_specs=[
            whole(valid.shape), whole(lora.shape),
            pl.BlockSpec((right.shape[0], PAIR), lambda i: (0, i)),
            pl.BlockSpec((1, PAIR), lambda i: (0, i)),
            column, column,
        ],
        out_specs=[column, piece, piece],
        out_shape=[
            jax.ShapeDtypeStruct((rows, width), f32),
            jax.ShapeDtypeStruct((reqs, pairs, PAIR, PAIR), bf16),
            jax.ShapeDtypeStruct((reqs, pairs, PAIR, PAIR), f32),
        ],
        compiler_params=pltpu.CompilerParams(vmem_limit_bytes=32 << 20),
        cost_estimate=pl.CostEstimate(flops=10**9, bytes_accessed=8 << 20, transcendentals=10**6),
        name="local_states",
    )(valid, lora, right, speed, k, v)


def within_chunk_stepwise(r, k, v, w):
    rows = lax.broadcasted_iota(jnp.int32, (CHUNK, 1), 0)
    ones = jnp.ones((CHUNK, PAIR), f32)
    keep = same_head()

    def token(t, carried):
        state, out = carried
        mine = rows == t
        dot = functools.partial(lax.dot_general, precision=HIGHEST, preferred_element_type=f32)
        out = out + dot(jnp.where(mine, r, 0.0), state, (((1,), (0,)), ((), ())))
        fade = jnp.exp(dot(jnp.where(mine, w, 0.0), ones, CONTRACT_ROWS))
        dyad = jnp.where(keep, dot(jnp.where(mine, k, 0.0), v, CONTRACT_ROWS), 0.0)
        return fade * state + dyad, out

    zero = jnp.zeros((PAIR, PAIR), f32)
    return lax.fori_loop(0, CHUNK, token, (zero, jnp.zeros((CHUNK, PAIR), f32)))[1]


def read_kernel(
    span, valid_ref, r_ref, k_ref, v_ref, w_ref, in_ref, l_ref, t_ref, reward_ref, scale_ref,
    out_ref, state_ref, inner,
):
    rows = k_ref.shape[0]
    keep = same_head()
    average = jnp.where(keep, 1.0, 0.0).astype(bf16)
    first_head = lax.broadcasted_iota(jnp.int32, (1, PAIR), 1) < ATTEND_DIM
    strict = earlier(CHUNK)
    strict = jnp.concatenate([strict, strict], axis=1)
    for b in range(rows // span):
        state = in_ref[b, 0]
        final = jnp.exp(t_ref[b, 0]) * state + l_ref[b, 0].astype(f32)
        state_ref[b, 0, 0] = final[:ATTEND_DIM, :ATTEND_DIM]
        state_ref[b, 0, 1] = final[ATTEND_DIM:, ATTEND_DIM:]
        for c in range(span // CHUNK):
            at = slice(b * span + c * CHUNK, b * span + (c + 1) * CHUNK)
            valid = valid_ref[at, 0:1]
            r, v = r_ref[at].astype(f32), v_ref[at]
            k = k_ref[at].astype(f32) * valid
            w = w_ref[at]
            before = sum_before(w)
            cum = before + w
            mid, last = before[CHUNK // 2 : CHUNK // 2 + 1], cum[CHUNK - 1 :]
            gentle = jnp.min(jnp.minimum(mid, last - mid)) > SAFE

            @pl.when(gentle)
            def _():
                query = (r * jnp.exp(before - mid)).astype(bf16)
                key = k * jnp.exp(mid - cum)
                keys = jnp.concatenate(
                    [jnp.where(first_head, key, 0.0), jnp.where(first_head, 0.0, key)], axis=0
                ).astype(bf16)
                scores = jnp.where(strict, dot32(query, keys, CONTRACT_LANES), 0.0).astype(bf16)
                value = v.astype(f32)
                values = jnp.concatenate(
                    [jnp.where(first_head, value, 0.0), jnp.where(first_head, 0.0, value)], axis=0
                ).astype(bf16)
                inner[...] = dot32(scores, values)

            @pl.when(jnp.logical_not(gentle))
            def _():
                inner[...] = within_chunk_stepwise(r, k, v.astype(f32), w)

            high, low = split_two(r * reward_ref[...] * k)
            own = (dot32(high, average) + dot32(low, average)) * v.astype(f32)
            y = inner[...] + own + dot32((r * jnp.exp(before)).astype(bf16), state.astype(bf16))
            if c + 1 < span // CHUNK:
                left_over = (k * jnp.exp(sum_after(w))).astype(bf16)
                grown = dot32(left_over, v, CONTRACT_ROWS)
                state = jnp.exp(column_total(w)) * state + jnp.where(keep, grown, 0.0)
            high, low = split_two(y)
            centred = y - (dot32(high, average) + dot32(low, average)) * (1.0 / ATTEND_DIM)
            high, low = split_two(centred * centred)
            spread = (dot32(high, average) + dot32(low, average)) * (1.0 / ATTEND_DIM)
            normed = centred * lax.rsqrt(spread + eps) * scale_ref[...] * valid
            out_ref[at] = normed.astype(bf16)


def read_states(valid, r, k, v, w, incoming, local_state, totals, reward, scale, span):
    rows, width = k.shape
    pairs, reqs = width // PAIR, rows // span
    column = pl.BlockSpec((rows, PAIR), lambda i: (0, i))
    line = pl.BlockSpec((1, PAIR), lambda i: (0, i))
    piece = pl.BlockSpec((reqs, 1, PAIR, PAIR), lambda i: (0, i, 0, 0))
    heads = pl.BlockSpec((reqs, 1, 2, ATTEND_DIM, ATTEND_DIM), lambda i: (0, i, 0, 0, 0))
    return pl.pallas_call(
        functools.partial(read_kernel, span),
        grid=(pairs,),
        in_specs=[
            pl.BlockSpec(valid.shape, lambda i: (0, 0)),
            column, column, column, column, piece, piece, piece, line, line,
        ],
        out_specs=[column, heads],
        out_shape=[
            jax.ShapeDtypeStruct((rows, width), bf16),
            jax.ShapeDtypeStruct((reqs, pairs, 2, ATTEND_DIM, ATTEND_DIM), f32),
        ],
        scratch_shapes=[pltpu.VMEM((CHUNK, PAIR), f32)],
        compiler_params=pltpu.CompilerParams(vmem_limit_bytes=32 << 20),
        cost_estimate=pl.CostEstimate(flops=2 * 10**9, bytes_accessed=8 << 20, transcendentals=10**6),
        name="read_states",
    )(valid, r, k, v, w, incoming, local_state, totals, reward, scale)


def local(
    incoming_activations,
    standardize_scaling,
    lagged_blending_weights,
    learner_line_permutation,
    learner_acceptor_lookup_slices,
    learner_projection_slices,
    fading_left_matrix,
    fading_right_matrix,
    feature_fading_speed,
    self_reward,
    cluster_scaling_vector,
    prompt_extents,
):
    reqs, span, width = incoming_activations.shape
    rows = reqs * span
    local_width = feature_fading_speed.shape[0]
    x = incoming_activations.reshape(rows, width)
    weight_out = lax.all_gather(
        learner_projection_slices.T.astype(bf16), ("req", "seq"), axis=0, tiled=True
    )
    positions = lax.axis_index("seq") * span + jnp.arange(span, dtype=jnp.int32)
    valid = (positions[None, :] < prompt_extents[:, None]).astype(f32).reshape(rows, 1)
    valid = jnp.broadcast_to(valid, (rows, PAIR))
    shard = learner_acceptor_lookup_slices.shape[1]
    perm = learner_line_permutation.reshape(SIDE * SIDE, SIDE, shard).transpose(1, 0, 2)
    projected, lora = project(
        x, incoming_activations[:, span - 1, :], perm.reshape(1, width),
        standardize_scaling[None], lagged_blending_weights, fading_left_matrix,
        learner_acceptor_lookup_slices,
    )
    r, k, v = projected
    decays, states, totals = local_states(
        valid, lora, fading_right_matrix, feature_fading_speed[None], k, v, span
    )
    incoming = jnp.zeros(states.shape, f32)
    sent = jnp.zeros_like(totals)
    for by in range(1, lax.axis_size("seq")):
        far_state = from_behind(states, "seq", by).astype(f32)
        incoming = incoming + jnp.exp(sent) * far_state
        if by + 1 < lax.axis_size("seq"):
            far_total = from_behind(totals[..., 0], "seq", by)
            sent = sent + far_total[..., None]
    normed, final = read_states(
        valid, r, k, v, decays, incoming, states, totals,
        self_reward[None], cluster_scaling_vector[None], span,
    )
    stretch_states = final.reshape(reqs, 1, local_width // ATTEND_DIM, ATTEND_DIM * ATTEND_DIM)
    terms = dot32(normed, weight_out, CONTRACT_LANES)
    summed = lax.psum_scatter(
        terms.astype(bf16), "tensor", scatter_dimension=1, tiled=True
    ).astype(f32)
    share = width // lax.axis_size("tensor")
    residual = lax.dynamic_slice_in_dim(x, lax.axis_index("tensor") * share, share, 1)
    hidden_out = (residual.astype(f32) + summed).astype(bf16).reshape(reqs, span, share)
    return (hidden_out, stretch_states)


def solution(mesh):
    in_specs = (
        P("req", "seq", None),
        P(),
        P(),
        P(),
        P(None, ("req", "seq"), "tensor"),
        P("tensor", ("req", "seq")),
        P(),
        P(None, "tensor"),
        P("tensor"),
        P("tensor"),
        P("tensor"),
        P("req"),
    )
    out_specs = (P("req", "seq", "tensor"), P("req", "seq", "tensor", None))
    return jax.shard_map(local, mesh=mesh, in_specs=in_specs, out_specs=out_specs, check_vma=False)
```

```python
import functools

import jax
import jax.numpy as jnp
from jax import lax
from jax.experimental import pallas as pl
from jax.experimental.pallas import tpu as pltpu
from jax.sharding import PartitionSpec as P

ATTEND_DIM = 64
PAIR = 128
CHUNK = 128
eps = 1e-05
f32 = jnp.float32
bf16 = jnp.bfloat16
CONTRACT_ROWS = (((0,), (0,)), ((), ()))
CONTRACT_LANES = (((1,), (1,)), ((), ()))


def split_two(value):
    high = value.astype(bf16)
    low = (value - high.astype(f32)).astype(bf16)
    return high, low


def dot32(a, b, dims=(((1,), (0,)), ((), ()))):
    return lax.dot_general(a, b, dims, preferred_element_type=f32)


MESH = pl.DeviceIdType.MESH
ORDERS = (("x", "y", "z"), ("y", "z", "x"), ("z", "x", "y"))
PLACES = (("z", "y", "x"), ("x", "y", "z"), ("y", "x", "z"))
SIDE = 4
STEP = 512


def position():
    req = lax.axis_index("req")
    return {"x": req // SIDE, "z": req % SIDE, "y": lax.axis_index("seq")}


def moved(at, axis, by):
    return {**at, axis: (at[axis] + by + SIDE) % SIDE}


def device(at):
    return (lax.axis_index("tensor"), at["x"] * SIDE + at["z"], at["y"])


def greet_neighbours(at):
    barrier = pltpu.get_barrier_semaphore()
    for axis in "xyz":
        for by in (1, -1):
            pl.semaphore_signal(
                barrier, inc=1, device_id=device(moved(at, axis, by)), device_id_type=MESH
            )
    pl.semaphore_wait(barrier, 6)


class Ring:
    def __init__(self, slots, order, places, send, recv, parts):
        self.slots, self.order, self.places = slots, order, places
        self.send, self.recv, self.parts = send, recv, parts
        self.at = position()

    def block(self, phase, where, part):
        index = []
        for axis in self.places:
            turn = self.order.index(axis)
            index.append(slice(None) if turn < phase else where if turn == phase else self.at[axis])
        return self.slots.at[(*index, *part)]

    def copy(self, phase, kind, right):
        axis = self.order[phase]
        to = moved(self.at, axis, 1 if right else -1)
        if kind == 0:
            ref = self.block(phase, self.at[axis], ())
        else:
            source = moved(self.at, axis, -1 if right else 1)[axis]
            ref = self.block(phase, source, (self.parts[0 if right else 1],))
        slot = 2 * kind + (0 if right else 1)
        return pltpu.make_async_remote_copy(
            ref, ref, self.send.at[phase, slot], self.recv.at[phase, slot],
            device_id=device(to), device_id_type=MESH,
        )

    def start(self, phase, kind):
        for right in (True, False):
            self.copy(phase, kind, right).start()

    def arrived(self, phase, kind):
        for right in (True, False):
            self.copy(phase, kind, right).wait_recv()

    def finish(self):
        for phase in range(3):
            for kind in range(2):
                for right in (True, False):
                    self.copy(phase, kind, right).wait_send()


def project_kernel(
    x_ref, last_ref, perm_ref, gain_ref, blend_ref, left_ref, w_ref, out_ref, lora_ref,
    slots, stack, mixed, chosen, picked, total, stats, low_rank, tail, load_sem, tail_sem, send, recv,
):
    rows, width = x_ref.shape
    reqs = last_ref.shape[0]
    span = rows // reqs
    at = position()
    half = w_ref.shape[1] // 2
    parts = (slice(0, half), slice(half, 2 * half))
    rings = [
        Ring(slots.at[m], ORDERS[m], PLACES[m], send.at[m], recv.at[m], parts) for m in range(3)
    ]
    load = pltpu.make_async_copy(x_ref, stack.at[pl.ds(0, rows)], load_sem)
    load.start()
    for m in range(3):
        slots[(m, *(at[axis] for axis in PLACES[m]))] = w_ref[m].astype(bf16)
    greet_neighbours(at)
    hand_on = pltpu.make_async_remote_copy(
        last_ref, tail, tail_sem.at[0], tail_sem.at[1],
        device_id=device(moved(at, "y", 1)), device_id_type=MESH,
    )
    hand_on.start()
    for ring in rings:
        ring.start(0, 0)

    table = jnp.concatenate([gain_ref[...], blend_ref[0:3, :]], axis=0)
    first = table.astype(bf16)
    rest = table - first.astype(f32)
    second = rest.astype(bf16)
    third = (rest - second.astype(f32)).astype(bf16)
    hand_on.wait_recv()
    before = jnp.where(at["y"] > 0, tail[...].astype(f32), 0.0).astype(bf16)
    pad = jnp.zeros((16 - reqs - 12, width), bf16)
    stack[rows:, :] = jnp.concatenate([before, first, second, third, pad], axis=0)
    low_rank[...] = jnp.zeros_like(low_rank)
    load.wait()

    def row_stats(i, _):
        here = pl.ds(pl.multiple_of(i * 16, 16), 16)
        part = stack[here, :].astype(f32)
        mean = jnp.mean(part, axis=-1, keepdims=True)
        centred = part - mean
        spread = jnp.mean(centred * centred, axis=-1, keepdims=True)
        stats[0, here, :] = jnp.broadcast_to(mean, (16, PAIR))
        stats[1, here, :] = jnp.broadcast_to(lax.rsqrt(spread + eps), (16, PAIR))
        return 0

    lax.fori_loop(0, stack.shape[0] // 16, row_stats, 0)

    def shifted(values, gain):
        mean, scale = stats[0, :, 0:1], stats[1, :, 0:1]
        row = lax.broadcasted_iota(jnp.int32, (rows, 1), 0)
        normal = (values - mean) * scale * gain
        current = normal[:rows]
        previous = pltpu.roll(current, 1, axis=0)
        for b in range(reqs):
            previous = jnp.where(row == b * span, normal[rows + b : rows + b + 1], previous)
        return current, previous - current

    piece = STEP // 2
    depth = chosen.shape[0]

    def mix_step(step, _):
        here = pl.ds(pl.multiple_of(step * STEP, STEP), STEP)
        names = perm_ref[:, here]
        picked[...] = jnp.zeros_like(picked)

        def pick(d, _):
            def one_hot(i, _):
                base = pl.multiple_of(i * 128, 128)
                feature = lax.broadcasted_iota(jnp.int32, (128, STEP), 0) + (base + d * depth)
                chosen[pl.ds(base, 128), :] = (feature == names).astype(f32).astype(bf16)
                return 0

            lax.fori_loop(0, depth // 128, one_hot, 0)
            source = stack[:, pl.ds(pl.multiple_of(d * depth, depth), depth)]
            picked[...] += dot32(source, chosen[...])
            return 0

        lax.fori_loop(0, width // depth, pick, 0)
        y, x0 = step // 2, (step % 2) * 2
        for i in range(2):
            values = picked[:, i * piece : (i + 1) * piece]
            own = values[rows + reqs :]
            own = own[0:4] + own[4:8] + own[8:12]
            current, delta = shifted(values, own[0:1])
            blended = [(current + delta * own[1 + j : 2 + j]).astype(bf16) for j in range(3)]
            picked[:rows, i * piece : (i + 1) * piece] = blended[0].astype(f32)
            mixed[1, x0 + i, :, pl.ds(pl.multiple_of(y * piece, piece), piece)] = blended[1]
            mixed[2, y, :, pl.ds(pl.multiple_of((x0 + i) * piece, piece), piece)] = blended[2]
        columns = pl.ds(pl.multiple_of(step * 128, 128), 128)
        for z in range(SIDE):
            pair = [picked[:rows, i * piece + z * 64 : i * piece + (z + 1) * 64] for i in range(2)]
            mixed[0, z, :, columns] = jnp.concatenate(pair, axis=1).astype(bf16)

        current, delta = shifted(stack[:, here].astype(f32), gain_ref[:, here])
        low_rank[...] += dot32(
            (current + delta * blend_ref[3:4, here]).astype(bf16),
            left_ref[pl.ds(pl.multiple_of(step * STEP, STEP), STEP), :],
        )

        @pl.when(step == 0)
        def _():
            for ring in rings:
                ring.arrived(0, 0)
                ring.start(0, 1)

        @pl.when(step == 1)
        def _():
            for ring in rings:
                ring.arrived(0, 1)
                ring.start(1, 0)

        @pl.when(step == 3)
        def _():
            for ring in rings:
                ring.arrived(1, 0)
                ring.start(1, 1)

        @pl.when(step == 4)
        def _():
            for ring in rings:
                ring.arrived(1, 1)
                ring.start(2, 0)

        return 0

    lax.fori_loop(0, width // STEP, mix_step, 0)
    lora_ref[...] = jnp.tanh(low_rank[...]).astype(bf16)

    def products(offset, fresh):
        def tile(i, _):
            m, n = i // 4, i % 4
            own = jnp.where(m == 0, at["z"], jnp.where(m == 1, at["x"], at["y"]))
            plane = (own + offset) % SIDE
            here = pl.ds(pl.multiple_of(n * 256, 256), 256)
            weight = slots[m, plane, :, :, :, here].reshape(width // SIDE, 256)
            product = dot32(mixed[m, plane], weight)
            if fresh:
                total[m, :, here] = product
            elif offset == 2:
                out_ref[m, :, here] = (total[m, :, here] + product).astype(bf16)
            else:
                total[m, :, here] += product
            return 0

        lax.fori_loop(0, 12, tile, 0)

    products(0, True)
    for ring in rings:
        ring.arrived(2, 0)
        ring.start(2, 1)
    products(1, False)
    products(3, False)
    for ring in rings:
        ring.arrived(2, 1)
    products(2, False)
    hand_on.wait_send()
    for ring in rings:
        ring.finish()


def project(x, last, perm, gain, blend, left, weights):
    rows, width = x.shape
    inner, local_width = left.shape[1], weights.shape[2]
    vmem = pl.BlockSpec(memory_space=pltpu.VMEM)
    return pl.pallas_call(
        project_kernel,
        in_specs=[pl.BlockSpec(memory_space=pl.ANY)] + [vmem] * 6,
        out_specs=[vmem, vmem],
        out_shape=[
            jax.ShapeDtypeStruct((3, rows, local_width), bf16),
            jax.ShapeDtypeStruct((rows, inner), bf16),
        ],
        scratch_shapes=[
            pltpu.VMEM((3, SIDE, SIDE, SIDE, *weights.shape[1:]), bf16),
            pltpu.VMEM((rows + 16, width), bf16),
            pltpu.VMEM((3, SIDE, rows, width // SIDE), bf16),
            pltpu.VMEM((width // 2, STEP), bf16),
            pltpu.VMEM((rows + 16, STEP), f32),
            pltpu.VMEM((3, rows, local_width), f32),
            pltpu.VMEM((2, rows + 16, PAIR), f32),
            pltpu.VMEM((rows, inner), f32),
            pltpu.VMEM(last.shape, bf16),
            pltpu.SemaphoreType.DMA,
            pltpu.SemaphoreType.DMA((2,)),
            pltpu.SemaphoreType.DMA((3, 3, 4)),
            pltpu.SemaphoreType.DMA((3, 3, 4)),
        ],
        compiler_params=pltpu.CompilerParams(
            collective_id=0, has_side_effects=True, vmem_limit_bytes=61 << 20
        ),
        cost_estimate=pl.CostEstimate(
            flops=100 * 10**9, bytes_accessed=32 << 20, transcendentals=0
        ),
        name="project",
    )(x, last, perm, gain, blend, left, weights)


def same_head():
    c = lax.broadcasted_iota(jnp.int32, (PAIR, PAIR), 0) // ATTEND_DIM
    v = lax.broadcasted_iota(jnp.int32, (PAIR, PAIR), 1) // ATTEND_DIM
    return c == v


LEVELS = 7
QUAD = 256
OUT_CUTS = (0, 384, 768, 1024)


def windows():
    t = lax.broadcasted_iota(jnp.int32, (CHUNK, QUAD), 0)
    s = lax.broadcasted_iota(jnp.int32, (CHUNK, QUAD), 1) % CHUNK
    chosen = [s < t, s > t]
    for level in range(LEVELS):
        middle = (((t >> (level + 1)) << 1) + 1) << level
        late = ((s >= middle) & (s < t)) & (t >= middle)
        early = ((s > t) & (s < middle)) & (t < middle)
        chosen.append(late | early)
    return [jnp.where(c, 1.0, 0.0).astype(bf16) for c in chosen]


def halves(values):
    first_head = lax.broadcasted_iota(jnp.int32, (1, PAIR), 1) < ATTEND_DIM
    return jnp.concatenate(
        [jnp.where(first_head, values, 0.0), jnp.where(first_head, 0.0, values)], axis=0
    ).astype(bf16)


def mixer_kernel(
    rkv_ref, lora_ref, right_ref, speed_ref, reward_ref, scale_ref, valid_ref, x_ref, w_ref,
    out_ref, state_ref,
    slots0, slots1, slots2, sums, level_of, decays, faded, y_buf, normed, expo,
    own_state, own_total, far_state, far_total, outgoing, incoming, residual,
    load_sem, send, recv, state_send, state_recv, total_send, total_recv, part_send, part_recv,
):
    rows, width = y_buf.shape
    reqs = own_state.shape[0]
    span = rows // reqs
    at = position()
    core = lax.axis_index("tensor")
    partner = (1 - core, lax.axis_index("req"), at["y"])
    share = x_ref.shape[1] // 2
    load = pltpu.make_async_copy(
        x_ref.at[:, pl.ds(pl.multiple_of(core * share, share), share)], residual, load_sem
    )
    load.start()
    half = w_ref.shape[0] // 2
    parts = (slice(0, half), slice(half, 2 * half))
    slots = (slots0, slots1, slots2)
    rings = []
    for i in range(3):
        slots[i][at["x"], at["z"], at["y"]] = w_ref[:, OUT_CUTS[i] : OUT_CUTS[i + 1]]
        rings.append(Ring(slots[i], ORDERS[i], ("x", "z", "y"), send.at[i], recv.at[i], parts))
    far_state[...] = jnp.zeros_like(far_state)
    far_total[...] = jnp.zeros_like(far_total)

    barrier = pltpu.get_barrier_semaphore()
    friends = [device(moved(at, axis, by)) for axis in "xyz" for by in (1, -1)]
    for friend in friends + [device(moved(at, "y", 2)), partner]:
        pl.semaphore_signal(barrier, inc=1, device_id=friend, device_id_type=MESH)
    pl.semaphore_wait(barrier, 8)
    for ring in rings:
        ring.start(0, 0)

    for i, window in enumerate(windows()):
        sums[i] = window
    t = lax.broadcasted_iota(jnp.int32, (CHUNK, QUAD), 0)
    s = lax.broadcasted_iota(jnp.int32, (CHUNK, QUAD), 1) % CHUNK
    level = jnp.full((CHUNK, QUAD), LEVELS, jnp.int32)
    for i in range(LEVELS):
        level = jnp.where(((t >> i) == (s >> i) + 1) & (((t >> i) & 1) == 1), i, level)
    level_of[...] = level
    keep = same_head()
    ones = jnp.where(keep, 1.0, 0.0).astype(bf16)
    head_sum = jnp.concatenate([ones, ones], axis=0)
    first_head = lax.broadcasted_iota(jnp.int32, (1, PAIR), 1) < ATTEND_DIM

    def over_head(values):
        return dot32(jnp.concatenate(split_two(values), axis=1), head_sum)

    def prepare(q, _):
        lanes = pl.ds(pl.multiple_of(q * QUAD, QUAD), QUAD)
        valid = valid_ref[:, 0:1]
        rate = jnp.exp(dot32(lora_ref[...], right_ref[:, lanes]))
        decays[:, lanes] = -speed_ref[:, lanes] * rate * valid
        for b in range(reqs):
            before, after, total = [], [], []
            for c in range(span // CHUNK):
                rows_c = slice(b * span + c * CHUNK, b * span + (c + 1) * CHUNK)
                w = decays[rows_c, lanes]
                both = jnp.concatenate(split_two(w), axis=0)
                before.append(dot32(sums[0], both))
                after.append(dot32(sums[1], both))
                total.append(before[c][CHUNK - 1 :] + w[CHUNK - 1 :])
            own_total[b : b + 1, lanes] = total[0] + total[1]
            at0 = slice(b * span, b * span + CHUNK)
            at1 = slice(b * span + CHUNK, (b + 1) * span)
            whole = slice(b * span, (b + 1) * span)
            r0, r1 = rkv_ref[0, at0, lanes].astype(f32), rkv_ref[0, at1, lanes].astype(f32)
            k0 = rkv_ref[1, at0, lanes].astype(f32) * valid[at0]
            k1 = rkv_ref[1, at1, lanes].astype(f32) * valid[at1]
            faded[at0, lanes] = (r0 * jnp.exp(before[0])).astype(bf16)
            faded[at1, lanes] = (r1 * jnp.exp(before[1] + total[0])).astype(bf16)
            query1 = (r1 * jnp.exp(before[1])).astype(bf16)
            key0 = (k0 * jnp.exp(after[0])).astype(bf16)
            keys = jnp.concatenate(
                [(k0 * jnp.exp(after[0] + total[1])).astype(bf16), (k1 * jnp.exp(after[1])).astype(bf16)],
                axis=0,
            )
            value = rkv_ref[2, whole, lanes]
            bonus0 = r0 * k0 * reward_ref[:, lanes]
            bonus1 = r1 * k1 * reward_ref[:, lanes]
            for p in range(2):
                pair = slice(p * PAIR, (p + 1) * PAIR)
                here = pl.ds(pl.multiple_of(q * QUAD + p * PAIR, PAIR), PAIR)
                grown = dot32(value[:, pair], keys[:, pair], CONTRACT_ROWS)
                own_state[b, 2 * q + p] = jnp.where(
                    first_head, grown[:ATTEND_DIM], grown[ATTEND_DIM:]
                ).astype(bf16)
                grown0 = dot32(value[:CHUNK, pair], key0[:, pair], CONTRACT_ROWS)
                grown0 = jnp.where(keep, grown0, 0.0).astype(bf16)
                y_buf[at0, here] = over_head(bonus0[:, pair]) * value[:CHUNK, pair].astype(f32)
                y_buf[at1, here] = over_head(bonus1[:, pair]) * value[CHUNK:, pair].astype(
                    f32
                ) + dot32(query1[:, pair], grown0, CONTRACT_LANES)

        @pl.when(q == 0)
        def _():
            for ring in rings:
                ring.arrived(0, 0)
                ring.start(0, 1)

        @pl.when(q == 1)
        def _():
            for ring in rings:
                ring.arrived(0, 1)
                ring.start(1, 0)

        @pl.when(q == 2)
        def _():
            for ring in rings:
                ring.arrived(1, 0)
                ring.start(1, 1)

        @pl.when(q == 3)
        def _():
            for ring in rings:
                ring.arrived(1, 1)
                ring.start(2, 0)

        return 0

    lax.fori_loop(0, width // QUAD, prepare, 0)

    def hand_on(by):
        to = device(moved(at, "y", by))
        return [
            pltpu.make_async_remote_copy(
                own, far.at[by - 1], s_sem.at[by - 1], r_sem.at[by - 1],
                device_id=to, device_id_type=MESH,
            )
            for own, far, s_sem, r_sem in (
                (own_state, far_state, state_send, state_recv),
                (own_total, far_total, total_send, total_recv),
            )
        ]

    for by in range(1, SIDE):
        @pl.when(at["y"] + by < SIDE)
        def _():
            for copy in hand_on(by):
                copy.start()

    def within(i, _):
        q, c = i // 4, i % 4
        lanes = pl.ds(pl.multiple_of(q * QUAD, QUAD), QUAD)
        rows_c = pl.ds(pl.multiple_of(c * CHUNK, CHUNK), CHUNK)
        both = jnp.concatenate(split_two(decays[rows_c, lanes]), axis=0)
        for n in range(LEVELS):
            expo[n] = dot32(sums[2 + n], both)
        row = lax.broadcasted_iota(jnp.int32, (CHUNK, 1), 0)
        valid = valid_ref[rows_c, 0:1]
        for p in range(2):
            pair = slice(p * PAIR, (p + 1) * PAIR)
            here = pl.ds(pl.multiple_of(q * QUAD + p * PAIR, PAIR), PAIR)
            r = rkv_ref[0, rows_c, here].astype(f32)
            k = rkv_ref[1, rows_c, here].astype(f32) * valid
            scores = jnp.zeros((CHUNK, QUAD), f32)
            for n in range(LEVELS):
                side = jnp.where(((row >> n) & 1) == 1, r, k) * jnp.exp(expo[n, :, pair])
                found = dot32(side.astype(bf16), halves(side), CONTRACT_LANES)
                scores = jnp.where(level_of[...] == n, found, scores)
            values = halves(rkv_ref[2, rows_c, here].astype(f32))
            y_buf[rows_c, here] += dot32(scores.astype(bf16), values)

        @pl.when(i == 10)
        def _():
            for ring in rings:
                ring.arrived(2, 0)
                ring.start(2, 1)

        return 0

    lax.fori_loop(0, width // QUAD * (rows // CHUNK), within, 0)

    for by in range(1, SIDE):
        @pl.when(at["y"] >= by)
        def _():
            for copy in hand_on(by):
                copy.wait_recv()

    def finish(p, _):
        here = pl.ds(pl.multiple_of(p * PAIR, PAIR), PAIR)
        for b in range(reqs):
            whole = slice(b * span, (b + 1) * span)
            near = far_total[0, b : b + 1, here]
            state = (
                far_state[0, b, p].astype(f32)
                + jnp.exp(near) * far_state[1, b, p].astype(f32)
                + jnp.exp(near + far_total[1, b : b + 1, here]) * far_state[2, b, p].astype(f32)
            )
            final = jnp.exp(own_total[b : b + 1, here]) * state + own_state[b, p].astype(f32)
            state_ref[b, p] = final.T
            y = y_buf[whole, here] + dot32(faded[whole, here], halves(state), CONTRACT_LANES)
            centred = y - over_head(y) * (1.0 / ATTEND_DIM)
            spread = over_head(centred * centred) * (1.0 / ATTEND_DIM)
            scaled = centred * lax.rsqrt(spread + eps) * scale_ref[:, here]
            normed[whole, here] = (scaled * valid_ref[whole, 0:1]).astype(bf16)
        return 0

    lax.fori_loop(0, width // PAIR, finish, 0)
    for ring in rings:
        ring.arrived(2, 1)

    def terms(side, j):
        product = None
        for i in range(3):
            weight = slots[i][2 * side + j // SIDE, j % SIDE]
            weight = weight.reshape(SIDE * weight.shape[1], weight.shape[2])
            part = dot32(normed[:, OUT_CUTS[i] : OUT_CUTS[i + 1]], weight, CONTRACT_LANES)
            product = part if product is None else product + part
        return product.astype(bf16)

    def exchange(j):
        return pltpu.make_async_remote_copy(
            outgoing.at[j], incoming.at[j], part_send.at[j], part_recv.at[j],
            device_id=partner, device_id_type=MESH,
        )

    def give(j, _):
        outgoing[j] = terms(1 - core, j)
        exchange(j).start()
        return 0

    lax.fori_loop(0, 8, give, 0)
    load.wait()

    def keep_own(j, _):
        here = pl.ds(pl.multiple_of(j * QUAD, QUAD), QUAD)
        mine = terms(core, j).astype(f32)
        exchange(j).wait_recv()
        summed = mine + incoming[j].astype(f32)
        out_ref[:, here] = (residual[:, here].astype(f32) + summed).astype(bf16)
        return 0

    lax.fori_loop(0, 8, keep_own, 0)

    def sent(j, _):
        exchange(j).wait_send()
        return 0

    lax.fori_loop(0, 8, sent, 0)
    for by in range(1, SIDE):
        @pl.when(at["y"] + by < SIDE)
        def _():
            for copy in hand_on(by):
                copy.wait_send()
    for ring in rings:
        ring.finish()


def mixer(rkv, lora, right, speed, reward, scale, valid, x, weight, reqs):
    rows, width = rkv.shape[1:]
    share = x.shape[1] // 2
    pairs = width // PAIR
    vmem = pl.BlockSpec(memory_space=pltpu.VMEM)
    dma = pltpu.SemaphoreType.DMA
    return pl.pallas_call(
        mixer_kernel,
        in_specs=[vmem] * 7 + [pl.BlockSpec(memory_space=pl.ANY), vmem],
        out_specs=[vmem, vmem],
        out_shape=[
            jax.ShapeDtypeStruct((rows, share), bf16),
            jax.ShapeDtypeStruct((reqs, pairs, PAIR, ATTEND_DIM), f32),
        ],
        scratch_shapes=[
            *(
                pltpu.VMEM((SIDE, SIDE, SIDE, weight.shape[0], OUT_CUTS[i + 1] - OUT_CUTS[i]), bf16)
                for i in range(3)
            ),
            pltpu.VMEM((2 + LEVELS, CHUNK, QUAD), bf16),
            pltpu.VMEM((CHUNK, QUAD), jnp.int32),
            pltpu.VMEM((rows, width), f32),
            pltpu.VMEM((rows, width), bf16),
            pltpu.VMEM((rows, width), f32),
            pltpu.VMEM((rows, width), bf16),
            pltpu.VMEM((LEVELS, CHUNK, QUAD), f32),
            pltpu.VMEM((reqs, pairs, ATTEND_DIM, PAIR), bf16),
            pltpu.VMEM((reqs, width), f32),
            pltpu.VMEM((3, reqs, pairs, ATTEND_DIM, PAIR), bf16),
            pltpu.VMEM((3, reqs, width), f32),
            pltpu.VMEM((8, rows, QUAD), bf16),
            pltpu.VMEM((8, rows, QUAD), bf16),
            pltpu.VMEM((rows, share), bf16),
            dma,
            dma((3, 3, 4)), dma((3, 3, 4)),
            dma((3,)), dma((3,)), dma((3,)), dma((3,)),
            dma((8,)), dma((8,)),
        ],
        compiler_params=pltpu.CompilerParams(
            collective_id=1, has_side_effects=True, vmem_limit_bytes=56 << 20
        ),
        cost_estimate=pl.CostEstimate(flops=40 * 10**9, bytes_accessed=32 << 20, transcendentals=0),
        name="mixer",
    )(rkv, lora, right, speed, reward, scale, valid, x, weight)


def local(
    incoming_activations,
    standardize_scaling,
    lagged_blending_weights,
    learner_line_permutation,
    learner_acceptor_lookup_slices,
    learner_projection_slices,
    fading_left_matrix,
    fading_right_matrix,
    feature_fading_speed,
    self_reward,
    cluster_scaling_vector,
    prompt_extents,
):
    reqs, span, width = incoming_activations.shape
    rows = reqs * span
    local_width = feature_fading_speed.shape[0]
    x = incoming_activations.reshape(rows, width)
    weight_out = learner_projection_slices.T.astype(bf16)
    positions = lax.axis_index("seq") * span + jnp.arange(span, dtype=jnp.int32)
    valid = (positions[None, :] < prompt_extents[:, None]).astype(f32).reshape(rows, 1)
    valid = jnp.broadcast_to(valid, (rows, PAIR))
    shard = learner_acceptor_lookup_slices.shape[1]
    perm = learner_line_permutation.reshape(SIDE * SIDE, SIDE, shard).transpose(1, 0, 2)
    projected, lora = project(
        x, incoming_activations[:, span - 1, :], perm.reshape(1, width),
        standardize_scaling[None], lagged_blending_weights, fading_left_matrix,
        learner_acceptor_lookup_slices,
    )
    hidden, final = mixer(
        projected, lora, fading_right_matrix, feature_fading_speed[None], self_reward[None],
        cluster_scaling_vector[None], valid, x, weight_out, reqs,
    )
    stretch_states = final.reshape(reqs, 1, local_width // ATTEND_DIM, ATTEND_DIM * ATTEND_DIM)
    return (hidden.reshape(reqs, span, hidden.shape[1]), stretch_states)


def solution(mesh):
    in_specs = (
        P("req", "seq", None),
        P(),
        P(),
        P(),
        P(None, ("req", "seq"), "tensor"),
        P("tensor", ("req", "seq")),
        P(),
        P(None, "tensor"),
        P("tensor"),
        P("tensor"),
        P("tensor"),
        P("req"),
    )
    out_specs = (P("req", "seq", "tensor"), P("req", "seq", "tensor", None))
    return jax.shard_map(local, mesh=mesh, in_specs=in_specs, out_specs=out_specs, check_vma=False)
```

```python
import functools

import jax
import jax.numpy as jnp
from jax import lax
from jax.experimental import pallas as pl
from jax.experimental.pallas import tpu as pltpu
from jax.sharding import PartitionSpec as P

ATTEND_DIM = 64
PAIR = 128
CHUNK = 128
eps = 1e-05
f32 = jnp.float32
bf16 = jnp.bfloat16
CONTRACT_ROWS = (((0,), (0,)), ((), ()))
CONTRACT_LANES = (((1,), (1,)), ((), ()))


def split_two(value):
    high = value.astype(bf16)
    low = (value - high.astype(f32)).astype(bf16)
    return high, low


def dot32(a, b, dims=(((1,), (0,)), ((), ()))):
    return lax.dot_general(a, b, dims, preferred_element_type=f32)


MESH = pl.DeviceIdType.MESH
ORDERS = (("x", "y", "z"), ("y", "z", "x"), ("z", "x", "y"))
PLACES = (("z", "y", "x"), ("x", "y", "z"), ("y", "x", "z"))
SIDE = 4
STEP = 512
OUT_CUTS = (0, 384, 768, 1024)


def position():
    req = lax.axis_index("req")
    return {"x": req // SIDE, "z": req % SIDE, "y": lax.axis_index("seq")}


def moved(at, axis, by):
    return {**at, axis: (at[axis] + by + SIDE) % SIDE}


def device(at):
    return (lax.axis_index("tensor"), at["x"] * SIDE + at["z"], at["y"])


def greet_neighbours(at):
    barrier = pltpu.get_barrier_semaphore()
    for axis in "xyz":
        for by in (1, -1):
            pl.semaphore_signal(
                barrier, inc=1, device_id=device(moved(at, axis, by)), device_id_type=MESH
            )
    pl.semaphore_wait(barrier, 6)


class Ring:
    def __init__(self, slots, order, places, send, recv, parts):
        self.slots, self.order, self.places = slots, order, places
        self.send, self.recv, self.parts = send, recv, parts
        self.at = position()

    def block(self, phase, where, part):
        index = []
        for axis in self.places:
            turn = self.order.index(axis)
            index.append(slice(None) if turn < phase else where if turn == phase else self.at[axis])
        return self.slots.at[(*index, *part)]

    def copy(self, phase, slot):
        axis = self.order[phase]
        right = slot in (0, 2, 4)
        part = 0 if slot in (0, 3, 4) else 1
        by = 1 if right else -1
        source = self.at if slot < 4 else moved(self.at, axis, -by)
        ref = self.block(phase, source[axis], (self.parts[part],))
        return pltpu.make_async_remote_copy(
            ref, ref, self.send.at[phase, slot], self.recv.at[phase, slot],
            device_id=device(moved(self.at, axis, by)), device_id_type=MESH,
        )

    def start(self, phase):
        for slot in range(4):
            self.copy(phase, slot).start()

    def turn(self, phase):
        for slot in range(2):
            self.copy(phase, slot).wait_recv()
            self.copy(phase, slot + 4).start()

    def near(self, phase):
        for slot in range(2, 4):
            self.copy(phase, slot).wait_recv()

    def far(self, phase):
        for slot in range(4, 6):
            self.copy(phase, slot).wait_recv()

    def settle(self, phase):
        self.near(phase)
        self.far(phase)

    def sent(self, phase):
        for slot in range(6):
            self.copy(phase, slot).wait_send()


def each(rings, *steps):
    for name, phase in steps:
        for ring in rings:
            getattr(ring, name)(phase)


def project_kernel(
    x_ref, perm_ref, gain_ref, blend_ref, left_ref, w_ref, w_out_ref,
    out_ref, lora_ref, plane0, plane1, plane2,
    slots, slots0, slots1, slots2, stack, mixed, chosen, picked, total, stats, low_rank, last, tail,
    load_sem, save_sem, tail_sem, send, recv, out_send, out_recv,
):
    rows, width = x_ref.shape
    reqs = last.shape[0]
    span = rows // reqs
    at = position()
    half = w_ref.shape[1] // 2
    parts = (slice(0, half), slice(half, 2 * half))
    rings = [
        Ring(slots.at[m], ORDERS[m], PLACES[m], send.at[m], recv.at[m], parts) for m in range(3)
    ]
    load = pltpu.make_async_copy(x_ref, stack.at[pl.ds(0, rows)], load_sem)
    load.start()
    for m in range(3):
        slots[(m, *(at[axis] for axis in PLACES[m]))] = w_ref[m].astype(bf16)
    greet_neighbours(at)
    each(rings, ("start", 0))
    load.wait()
    for b in range(reqs):
        end = (b + 1) * span
        last[b : b + 1, :] = stack[end - 16 : end, :].astype(f32)[15:16].astype(bf16)
    hand_on = pltpu.make_async_remote_copy(
        last, tail, tail_sem.at[0], tail_sem.at[1],
        device_id=device(moved(at, "y", 1)), device_id_type=MESH,
    )
    hand_on.start()

    out_slots = (slots0, slots1, slots2)
    out_rings = []
    turned = w_out_ref[...].T.astype(bf16)
    for i in range(3):
        places = tuple(axis for axis in "xzy" if axis != ORDERS[i][2])
        out_slots[i][tuple(at[axis] for axis in places)] = turned[:, OUT_CUTS[i] : OUT_CUTS[i + 1]]
        out_rings.append(Ring(out_slots[i], ORDERS[i], places, out_send.at[i], out_recv.at[i], parts))

    table = jnp.concatenate([gain_ref[...], blend_ref[0:3, :]], axis=0)
    first = table.astype(bf16)
    rest = table - first.astype(f32)
    second = rest.astype(bf16)
    third = (rest - second.astype(f32)).astype(bf16)
    each(rings, ("turn", 0))
    hand_on.wait_recv()
    before = jnp.where(at["y"] > 0, tail[...].astype(f32), 0.0).astype(bf16)
    pad = jnp.zeros((16 - reqs - 12, width), bf16)
    stack[rows:, :] = jnp.concatenate([before, first, second, third, pad], axis=0)
    low_rank[...] = jnp.zeros_like(low_rank)

    def row_stats(i, _):
        here = pl.ds(pl.multiple_of(i * 16, 16), 16)
        part = stack[here, :].astype(f32)
        mean = jnp.mean(part, axis=-1, keepdims=True)
        centred = part - mean
        spread = jnp.mean(centred * centred, axis=-1, keepdims=True)
        stats[0, here, :] = jnp.broadcast_to(mean, (16, PAIR))
        stats[1, here, :] = jnp.broadcast_to(lax.rsqrt(spread + eps), (16, PAIR))
        return 0

    lax.fori_loop(0, stack.shape[0] // 16, row_stats, 0)
    each(rings, ("settle", 0), ("start", 1))

    def shifted(values, gain):
        mean, scale = stats[0, :, 0:1], stats[1, :, 0:1]
        row = lax.broadcasted_iota(jnp.int32, (rows, 1), 0)
        normal = (values - mean) * scale * gain
        current = normal[:rows]
        previous = pltpu.roll(current, 1, axis=0)
        for b in range(reqs):
            previous = jnp.where(row == b * span, normal[rows + b : rows + b + 1], previous)
        return current, previous - current

    piece = STEP // 2
    depth = chosen.shape[0]

    def mix_step(step, _):
        here = pl.ds(pl.multiple_of(step * STEP, STEP), STEP)
        y, x0 = step // 2, (step % 2) * 2
        names = []
        for i in range(2):
            for z in range(0, SIDE, 2):
                at_row = (x0 + i) * 8 + z * 2 + y // 2
                low, high = perm_ref[pl.ds(at_row, 1), :], perm_ref[pl.ds(at_row + 2, 1), :]
                low_up, high_up = pltpu.roll(low, 64, axis=1), pltpu.roll(high, 64, axis=1)
                even = y % 2 == 0
                names.append(
                    jnp.where(
                        lax.broadcasted_iota(jnp.int32, (1, 128), 1) < 64,
                        jnp.where(even, low, low_up), jnp.where(even, high_up, high),
                    )
                )
        names = jnp.concatenate(names, axis=1)
        picked[...] = jnp.zeros_like(picked)

        def pick(d, _):
            def one_hot(i, _):
                base = pl.multiple_of(i * 128, 128)
                feature = lax.broadcasted_iota(jnp.int32, (128, STEP), 0) + (base + d * depth)
                chosen[pl.ds(base, 128), :] = (feature == names).astype(f32).astype(bf16)
                return 0

            lax.fori_loop(0, depth // 128, one_hot, 0)
            source = stack[:, pl.ds(pl.multiple_of(d * depth, depth), depth)]
            picked[...] += dot32(source, chosen[...])
            return 0

        lax.fori_loop(0, width // depth, pick, 0)
        for i in range(2):
            values = picked[:, i * piece : (i + 1) * piece]
            own = values[rows + reqs :]
            own = own[0:4] + own[4:8] + own[8:12]
            current, delta = shifted(values, own[0:1])
            blended = [(current + delta * own[1 + j : 2 + j]).astype(bf16) for j in range(3)]
            picked[:rows, i * piece : (i + 1) * piece] = blended[0].astype(f32)
            mixed[1, x0 + i, :, pl.ds(pl.multiple_of(y * piece, piece), piece)] = blended[1]
            mixed[2, y, :, pl.ds(pl.multiple_of((x0 + i) * piece, piece), piece)] = blended[2]
        columns = pl.ds(pl.multiple_of(step * 128, 128), 128)
        for z in range(SIDE):
            pair = [picked[:rows, i * piece + z * 64 : i * piece + (z + 1) * 64] for i in range(2)]
            mixed[0, z, :, columns] = jnp.concatenate(pair, axis=1).astype(bf16)

        current, delta = shifted(stack[:, here].astype(f32), gain_ref[:, here])
        low_rank[...] += dot32(
            (current + delta * blend_ref[3:4, here]).astype(bf16),
            left_ref[pl.ds(pl.multiple_of(step * STEP, STEP), STEP), :],
        )

        for when, group, steps in (
            (0, rings, (("turn", 1),)),
            (2, rings, (("settle", 1), ("start", 2))),
            (3, out_rings, (("start", 0),)),
            (4, out_rings, (("turn", 0),)),
            (5, out_rings, (("settle", 0), ("start", 1))),
            (7, out_rings, (("turn", 1),)),
            (7, rings, (("turn", 2),)),
        ):
            @pl.when(step == when)
            def _():
                each(group, *steps)

        return 0

    lax.fori_loop(0, width // STEP, mix_step, 0)
    lora_ref[...] = jnp.tanh(low_rank[...]).astype(bf16)

    def products(offset, fresh):
        def tile(i, _):
            m, n = i // 4, i % 4
            own = jnp.where(m == 0, at["z"], jnp.where(m == 1, at["x"], at["y"]))
            plane = (own + offset) % SIDE
            here = pl.ds(pl.multiple_of(n * 256, 256), 256)
            weight = slots[m, plane, :, :, :, here].reshape(width // SIDE, 256)
            product = dot32(mixed[m, plane], weight)
            if fresh:
                total[m, :, here] = product
            elif offset == 2:
                out_ref[m, :, here] = (total[m, :, here] + product).astype(bf16)
            else:
                total[m, :, here] += product
            return 0

        lax.fori_loop(0, 12, tile, 0)

    products(0, True)
    each(rings, ("near", 2))
    products(1, False)
    products(3, False)
    each(out_rings, ("settle", 1))
    saves = [
        pltpu.make_async_copy(kept, plane, save_sem.at[i])
        for i, (plane, kept) in enumerate(zip((plane0, plane1, plane2), out_slots))
    ]
    for save in saves:
        save.start()
    each(rings, ("far", 2))
    products(2, False)
    hand_on.wait_send()
    for save in saves:
        save.wait()
    each(rings, ("sent", 0), ("sent", 1), ("sent", 2))
    each(out_rings, ("sent", 0), ("sent", 1))


def project(x, reqs, perm, gain, blend, left, weights, out_weight):
    rows, width = x.shape
    shard = weights.shape[1]
    cuts = [OUT_CUTS[i + 1] - OUT_CUTS[i] for i in range(3)]
    dma = pltpu.SemaphoreType.DMA
    inner, local_width = left.shape[1], weights.shape[2]
    vmem = pl.BlockSpec(memory_space=pltpu.VMEM)
    return pl.pallas_call(
        project_kernel,
        in_specs=[pl.BlockSpec(memory_space=pl.ANY)] + [vmem] * 6,
        out_specs=[vmem] * 2 + [pl.BlockSpec(memory_space=pl.ANY)] * 3,
        out_shape=[
            jax.ShapeDtypeStruct((3, rows, local_width), bf16),
            jax.ShapeDtypeStruct((rows, inner), bf16),
            *(jax.ShapeDtypeStruct((SIDE, SIDE, shard, cut), bf16) for cut in cuts),
        ],
        scratch_shapes=[
            pltpu.VMEM((3, SIDE, SIDE, SIDE, *weights.shape[1:]), bf16),
            *(pltpu.VMEM((SIDE, SIDE, shard, cut), bf16) for cut in cuts),
            pltpu.VMEM((rows + 16, width), bf16),
            pltpu.VMEM((3, SIDE, rows, width // SIDE), bf16),
            pltpu.VMEM((width // 4, STEP), bf16),
            pltpu.VMEM((rows + 16, STEP), f32),
            pltpu.VMEM((3, rows, local_width), f32),
            pltpu.VMEM((2, rows + 16, PAIR), f32),
            pltpu.VMEM((rows, inner), f32),
            pltpu.VMEM((reqs, width), bf16),
            pltpu.VMEM((reqs, width), bf16),
            dma, dma((3,)), dma((2,)),
            dma((3, 3, 6)), dma((3, 3, 6)), dma((3, 2, 6)), dma((3, 2, 6)),
        ],
        compiler_params=pltpu.CompilerParams(
            collective_id=0, has_side_effects=True, vmem_limit_bytes=61 << 20
        ),
        cost_estimate=pl.CostEstimate(
            flops=100 * 10**9, bytes_accessed=32 << 20, transcendentals=0
        ),
        name="project",
    )(x, perm, gain, blend, left, weights, out_weight)


def same_head():
    c = lax.broadcasted_iota(jnp.int32, (PAIR, PAIR), 0) // ATTEND_DIM
    v = lax.broadcasted_iota(jnp.int32, (PAIR, PAIR), 1) // ATTEND_DIM
    return c == v


LEVELS = 7
QUAD = 256


def windows():
    t = lax.broadcasted_iota(jnp.int32, (CHUNK, QUAD), 0)
    s = lax.broadcasted_iota(jnp.int32, (CHUNK, QUAD), 1) % CHUNK
    chosen = [s < t, s > t]
    for level in range(LEVELS):
        middle = (((t >> (level + 1)) << 1) + 1) << level
        late = ((s >= middle) & (s < t)) & (t >= middle)
        early = ((s > t) & (s < middle)) & (t < middle)
        chosen.append(late | early)
    return [jnp.where(c, 1.0, 0.0).astype(bf16) for c in chosen]


def halves(values):
    first_head = lax.broadcasted_iota(jnp.int32, (1, PAIR), 1) < ATTEND_DIM
    return jnp.concatenate(
        [jnp.where(first_head, values, 0.0), jnp.where(first_head, 0.0, values)], axis=0
    ).astype(bf16)


def mixer_kernel(
    extents_ref, rkv_ref, lora_ref, right_ref, speed_ref, reward_ref, scale_ref, x_ref,
    plane0, plane1, plane2,
    out_ref, state_ref,
    slots0, slots1, slots2, valid_ref, sums, level_of, decays, faded, y_buf, normed, expo,
    own_state, own_total, far_state, far_total, outgoing, incoming, residual,
    load_sem, plane_sem, send, recv, state_send, state_recv, total_send, total_recv, part_send, part_recv,
):
    rows, width = y_buf.shape
    reqs = own_state.shape[0]
    span = rows // reqs
    at = position()
    core = lax.axis_index("tensor")
    partner = (1 - core, lax.axis_index("req"), at["y"])
    share = x_ref.shape[1] // 2
    load = pltpu.make_async_copy(
        x_ref.at[:, pl.ds(pl.multiple_of(core * share, share), share)], residual, load_sem
    )
    load.start()
    half = plane0.shape[2] // 2
    parts = (slice(0, half), slice(half, 2 * half))
    slots = (slots0, slots1, slots2)
    rings = []
    for i in range(3):
        rings.append(Ring(slots[i], ORDERS[i], ("x", "z", "y"), send.at[i], recv.at[i], parts))
    fills = []
    for i, plane in enumerate((plane0, plane1, plane2)):
        own = rings[i].block(2, at[ORDERS[i][2]], ())
        fills.append(pltpu.make_async_copy(plane, own, plane_sem.at[i]))
        fills[i].start()
    far_state[...] = jnp.zeros_like(far_state)
    far_total[...] = jnp.zeros_like(far_total)

    barrier = pltpu.get_barrier_semaphore()
    friends = [device(moved(at, axis, by)) for axis in "xyz" for by in (1, -1)]
    for friend in friends + [device(moved(at, "y", 2)), partner]:
        pl.semaphore_signal(barrier, inc=1, device_id=friend, device_id_type=MESH)
    pl.semaphore_wait(barrier, 8)
    for fill in fills:
        fill.wait()
    each(rings, ("start", 2))
    row = lax.broadcasted_iota(jnp.int32, (rows, PAIR), 0)
    token = at["y"] * span + row % span
    inside = jnp.zeros((rows, PAIR), f32)
    for b in range(reqs):
        inside = jnp.where((row // span == b) & (token < extents_ref[b]), 1.0, inside)
    valid_ref[...] = inside

    for i, window in enumerate(windows()):
        sums[i] = window
    t = lax.broadcasted_iota(jnp.int32, (CHUNK, QUAD), 0)
    s = lax.broadcasted_iota(jnp.int32, (CHUNK, QUAD), 1) % CHUNK
    level = jnp.full((CHUNK, QUAD), LEVELS, jnp.int32)
    for i in range(LEVELS):
        level = jnp.where(((t >> i) == (s >> i) + 1) & (((t >> i) & 1) == 1), i, level)
    level_of[...] = level
    keep = same_head()
    ones = jnp.where(keep, 1.0, 0.0).astype(bf16)
    head_sum = jnp.concatenate([ones, ones], axis=0)
    first_head = lax.broadcasted_iota(jnp.int32, (1, PAIR), 1) < ATTEND_DIM

    def over_head(values):
        return dot32(jnp.concatenate(split_two(values), axis=1), head_sum)

    def prepare(q, _):
        lanes = pl.ds(pl.multiple_of(q * QUAD, QUAD), QUAD)
        valid = valid_ref[:, 0:1]
        rate = jnp.exp(dot32(lora_ref[...], right_ref[:, lanes]))
        decays[:, lanes] = -speed_ref[:, lanes] * rate * valid
        for b in range(reqs):
            before, after, total = [], [], []
            for c in range(span // CHUNK):
                rows_c = slice(b * span + c * CHUNK, b * span + (c + 1) * CHUNK)
                w = decays[rows_c, lanes]
                both = jnp.concatenate(split_two(w), axis=0)
                before.append(dot32(sums[0], both))
                after.append(dot32(sums[1], both))
                total.append(before[c][CHUNK - 1 :] + w[CHUNK - 1 :])
            own_total[b : b + 1, lanes] = total[0] + total[1]
            at0 = slice(b * span, b * span + CHUNK)
            at1 = slice(b * span + CHUNK, (b + 1) * span)
            whole = slice(b * span, (b + 1) * span)
            r0, r1 = rkv_ref[0, at0, lanes].astype(f32), rkv_ref[0, at1, lanes].astype(f32)
            k0 = rkv_ref[1, at0, lanes].astype(f32) * valid[at0]
            k1 = rkv_ref[1, at1, lanes].astype(f32) * valid[at1]
            faded[at0, lanes] = (r0 * jnp.exp(before[0])).astype(bf16)
            faded[at1, lanes] = (r1 * jnp.exp(before[1] + total[0])).astype(bf16)
            query1 = (r1 * jnp.exp(before[1])).astype(bf16)
            key0 = (k0 * jnp.exp(after[0])).astype(bf16)
            keys = jnp.concatenate(
                [(k0 * jnp.exp(after[0] + total[1])).astype(bf16), (k1 * jnp.exp(after[1])).astype(bf16)],
                axis=0,
            )
            value = rkv_ref[2, whole, lanes]
            bonus0 = r0 * k0 * reward_ref[:, lanes]
            bonus1 = r1 * k1 * reward_ref[:, lanes]
            for p in range(2):
                pair = slice(p * PAIR, (p + 1) * PAIR)
                here = pl.ds(pl.multiple_of(q * QUAD + p * PAIR, PAIR), PAIR)
                grown = dot32(value[:, pair], keys[:, pair], CONTRACT_ROWS)
                own_state[b, 2 * q + p] = jnp.where(
                    first_head, grown[:ATTEND_DIM], grown[ATTEND_DIM:]
                ).astype(bf16)
                grown0 = dot32(value[:CHUNK, pair], key0[:, pair], CONTRACT_ROWS)
                grown0 = jnp.where(keep, grown0, 0.0).astype(bf16)
                y_buf[at0, here] = over_head(bonus0[:, pair]) * value[:CHUNK, pair].astype(f32)
                y_buf[at1, here] = over_head(bonus1[:, pair]) * value[CHUNK:, pair].astype(
                    f32
                ) + dot32(query1[:, pair], grown0, CONTRACT_LANES)

        return 0

    lax.fori_loop(0, width // QUAD, prepare, 0)

    def hand_on(by):
        to = device(moved(at, "y", by))
        return [
            pltpu.make_async_remote_copy(
                own, far.at[by - 1], s_sem.at[by - 1], r_sem.at[by - 1],
                device_id=to, device_id_type=MESH,
            )
            for own, far, s_sem, r_sem in (
                (own_state, far_state, state_send, state_recv),
                (own_total, far_total, total_send, total_recv),
            )
        ]

    for by in range(1, SIDE):
        @pl.when(at["y"] + by < SIDE)
        def _():
            for copy in hand_on(by):
                copy.start()

    def within(i, _):
        q, c = i // 4, i % 4
        lanes = pl.ds(pl.multiple_of(q * QUAD, QUAD), QUAD)
        rows_c = pl.ds(pl.multiple_of(c * CHUNK, CHUNK), CHUNK)
        both = jnp.concatenate(split_two(decays[rows_c, lanes]), axis=0)
        for n in range(LEVELS):
            expo[n] = dot32(sums[2 + n], both)
        row = lax.broadcasted_iota(jnp.int32, (CHUNK, 1), 0)
        valid = valid_ref[rows_c, 0:1]
        for p in range(2):
            pair = slice(p * PAIR, (p + 1) * PAIR)
            here = pl.ds(pl.multiple_of(q * QUAD + p * PAIR, PAIR), PAIR)
            r = rkv_ref[0, rows_c, here].astype(f32)
            k = rkv_ref[1, rows_c, here].astype(f32) * valid
            scores = jnp.zeros((CHUNK, QUAD), f32)
            for n in range(LEVELS):
                side = jnp.where(((row >> n) & 1) == 1, r, k) * jnp.exp(expo[n, :, pair])
                found = dot32(side.astype(bf16), halves(side), CONTRACT_LANES)
                scores = jnp.where(level_of[...] == n, found, scores)
            values = halves(rkv_ref[2, rows_c, here].astype(f32))
            y_buf[rows_c, here] += dot32(scores.astype(bf16), values)

        @pl.when(i == 3)
        def _():
            each(rings, ("turn", 2))

        return 0

    lax.fori_loop(0, width // QUAD * (rows // CHUNK), within, 0)

    for by in range(1, SIDE):
        @pl.when(at["y"] >= by)
        def _():
            for copy in hand_on(by):
                copy.wait_recv()

    def finish(p, _):
        here = pl.ds(pl.multiple_of(p * PAIR, PAIR), PAIR)
        for b in range(reqs):
            whole = slice(b * span, (b + 1) * span)
            near = far_total[0, b : b + 1, here]
            state = (
                far_state[0, b, p].astype(f32)
                + jnp.exp(near) * far_state[1, b, p].astype(f32)
                + jnp.exp(near + far_total[1, b : b + 1, here]) * far_state[2, b, p].astype(f32)
            )
            final = jnp.exp(own_total[b : b + 1, here]) * state + own_state[b, p].astype(f32)
            state_ref[b, p] = final.T
            y = y_buf[whole, here] + dot32(faded[whole, here], halves(state), CONTRACT_LANES)
            centred = y - over_head(y) * (1.0 / ATTEND_DIM)
            spread = over_head(centred * centred) * (1.0 / ATTEND_DIM)
            scaled = centred * lax.rsqrt(spread + eps) * scale_ref[:, here]
            normed[whole, here] = (scaled * valid_ref[whole, 0:1]).astype(bf16)
        return 0

    lax.fori_loop(0, width // PAIR, finish, 0)
    each(rings, ("settle", 2))

    def terms(side, j):
        product = None
        for i in range(3):
            weight = slots[i][2 * side + j // SIDE, j % SIDE]
            weight = weight.reshape(SIDE * weight.shape[1], weight.shape[2])
            part = dot32(normed[:, OUT_CUTS[i] : OUT_CUTS[i + 1]], weight, CONTRACT_LANES)
            product = part if product is None else product + part
        return product.astype(bf16)

    def exchange(j):
        return pltpu.make_async_remote_copy(
            outgoing.at[j], incoming.at[j], part_send.at[j], part_recv.at[j],
            device_id=partner, device_id_type=MESH,
        )

    def give(j, _):
        outgoing[j] = terms(1 - core, j)
        exchange(j).start()
        return 0

    lax.fori_loop(0, 8, give, 0)
    load.wait()

    def keep_own(j, _):
        here = pl.ds(pl.multiple_of(j * QUAD, QUAD), QUAD)
        mine = terms(core, j).astype(f32)
        exchange(j).wait_recv()
        summed = mine + incoming[j].astype(f32)
        out_ref[:, here] = (residual[:, here].astype(f32) + summed).astype(bf16)
        return 0

    lax.fori_loop(0, 8, keep_own, 0)

    def sent(j, _):
        exchange(j).wait_send()
        return 0

    lax.fori_loop(0, 8, sent, 0)
    for by in range(1, SIDE):
        @pl.when(at["y"] + by < SIDE)
        def _():
            for copy in hand_on(by):
                copy.wait_send()
    each(rings, ("sent", 2))


def mixer(extents, rkv, lora, right, speed, reward, scale, x, planes):
    rows, width = rkv.shape[1:]
    share, reqs, shard = x.shape[1] // 2, extents.shape[0], planes[0].shape[2]
    pairs = width // PAIR
    vmem = pl.BlockSpec(memory_space=pltpu.VMEM)
    away = pl.BlockSpec(memory_space=pl.ANY)
    dma = pltpu.SemaphoreType.DMA
    return pl.pallas_call(
        mixer_kernel,
        in_specs=[pl.BlockSpec(memory_space=pltpu.SMEM)] + [vmem] * 6 + [away] * 4,
        out_specs=[vmem, vmem],
        out_shape=[
            jax.ShapeDtypeStruct((rows, share), bf16),
            jax.ShapeDtypeStruct((reqs, pairs, PAIR, ATTEND_DIM), f32),
        ],
        scratch_shapes=[
            *(
                pltpu.VMEM((SIDE, SIDE, SIDE, shard, OUT_CUTS[i + 1] - OUT_CUTS[i]), bf16)
                for i in range(3)
            ),
            pltpu.VMEM((rows, PAIR), f32),
            pltpu.VMEM((2 + LEVELS, CHUNK, QUAD), bf16),
            pltpu.VMEM((CHUNK, QUAD), jnp.int32),
            pltpu.VMEM((rows, width), f32),
            pltpu.VMEM((rows, width), bf16),
            pltpu.VMEM((rows, width), f32),
            pltpu.VMEM((rows, width), bf16),
            pltpu.VMEM((LEVELS, CHUNK, QUAD), f32),
            pltpu.VMEM((reqs, pairs, ATTEND_DIM, PAIR), bf16),
            pltpu.VMEM((reqs, width), f32),
            pltpu.VMEM((3, reqs, pairs, ATTEND_DIM, PAIR), bf16),
            pltpu.VMEM((3, reqs, width), f32),
            pltpu.VMEM((8, rows, QUAD), bf16),
            pltpu.VMEM((8, rows, QUAD), bf16),
            pltpu.VMEM((rows, share), bf16),
            dma, dma((3,)),
            dma((3, 3, 6)), dma((3, 3, 6)),
            dma((3,)), dma((3,)), dma((3,)), dma((3,)),
            dma((8,)), dma((8,)),
        ],
        compiler_params=pltpu.CompilerParams(
            collective_id=1, has_side_effects=True, vmem_limit_bytes=56 << 20
        ),
        cost_estimate=pl.CostEstimate(flops=40 * 10**9, bytes_accessed=32 << 20, transcendentals=0),
        name="mixer",
    )(extents, rkv, lora, right, speed, reward, scale, x, *planes)


def local(
    incoming_activations,
    standardize_scaling,
    lagged_blending_weights,
    learner_line_permutation,
    learner_acceptor_lookup_slices,
    learner_projection_slices,
    fading_left_matrix,
    fading_right_matrix,
    feature_fading_speed,
    self_reward,
    cluster_scaling_vector,
    prompt_extents,
):
    reqs, span, width = incoming_activations.shape
    rows = reqs * span
    local_width = feature_fading_speed.shape[0]
    x = incoming_activations.reshape(rows, width)
    projected, lora, *planes = project(
        x, reqs, learner_line_permutation.reshape(width // PAIR, PAIR), standardize_scaling[None],
        lagged_blending_weights, fading_left_matrix, learner_acceptor_lookup_slices,
        learner_projection_slices,
    )
    hidden, final = mixer(
        prompt_extents, projected, lora, fading_right_matrix, feature_fading_speed[None],
        self_reward[None], cluster_scaling_vector[None], x, planes,
    )
    stretch_states = final.reshape(reqs, 1, local_width // ATTEND_DIM, ATTEND_DIM * ATTEND_DIM)
    return (hidden.reshape(reqs, span, hidden.shape[1]), stretch_states)


def solution(mesh):
    in_specs = (
        P("req", "seq", None),
        P(),
        P(),
        P(),
        P(None, ("req", "seq"), "tensor"),
        P("tensor", ("req", "seq")),
        P(),
        P(None, "tensor"),
        P("tensor"),
        P("tensor"),
        P("tensor"),
        P("req"),
    )
    out_specs = (P("req", "seq", "tensor"), P("req", "seq", "tensor", None))
    return jax.shard_map(local, mesh=mesh, in_specs=in_specs, out_specs=out_specs, check_vma=False)
```

```python
import functools

import jax
import jax.numpy as jnp
from jax import lax
from jax.experimental import pallas as pl
from jax.experimental.pallas import tpu as pltpu
from jax.sharding import PartitionSpec as P

ATTEND_DIM = 64
PAIR = 128
CHUNK = 128
eps = 1e-05
f32 = jnp.float32
bf16 = jnp.bfloat16
CONTRACT_ROWS = (((0,), (0,)), ((), ()))
CONTRACT_LANES = (((1,), (1,)), ((), ()))


def split_two(value):
    high = value.astype(bf16)
    low = (value - high.astype(f32)).astype(bf16)
    return high, low


def dot32(a, b, dims=(((1,), (0,)), ((), ()))):
    return lax.dot_general(a, b, dims, preferred_element_type=f32)


MESH = pl.DeviceIdType.MESH
ORDERS = (("x", "y", "z"), ("y", "z", "x"), ("z", "x", "y"))
PLACES = (("z", "y", "x"), ("x", "y", "z"), ("y", "x", "z"))
SIDE = 4
STEP = 512
OUT_CUTS = (0, 384, 768, 1024)


def position():
    req = lax.axis_index("req")
    return {"x": req // SIDE, "z": req % SIDE, "y": lax.axis_index("seq")}


def moved(at, axis, by):
    return {**at, axis: (at[axis] + by + SIDE) % SIDE}


def device(at):
    return (lax.axis_index("tensor"), at["x"] * SIDE + at["z"], at["y"])


class Ring:
    def __init__(self, slots, order, places, send, recv, parts):
        self.slots, self.order, self.places = slots, order, places
        self.send, self.recv, self.parts = send, recv, parts
        self.at = position()

    def block(self, phase, where, part):
        index = []
        for axis in self.places:
            turn = self.order.index(axis)
            index.append(slice(None) if turn < phase else where if turn == phase else self.at[axis])
        return self.slots.at[(*index, *part)]

    def copy(self, phase, slot):
        axis = self.order[phase]
        right = slot in (0, 2, 4)
        part = 0 if slot in (0, 3, 4) else 1
        by = 1 if right else -1
        source = self.at if slot < 4 else moved(self.at, axis, -by)
        ref = self.block(phase, source[axis], (self.parts[part],))
        return pltpu.make_async_remote_copy(
            ref, ref, self.send.at[phase, slot], self.recv.at[phase, slot],
            device_id=device(moved(self.at, axis, by)), device_id_type=MESH,
        )

    def start(self, phase):
        for slot in range(4):
            self.copy(phase, slot).start()

    def turn(self, phase):
        for slot in range(2):
            self.copy(phase, slot).wait_recv()
            self.copy(phase, slot + 4).start()

    def near(self, phase):
        for slot in range(2, 4):
            self.copy(phase, slot).wait_recv()

    def far(self, phase):
        for slot in range(4, 6):
            self.copy(phase, slot).wait_recv()

    def settle(self, phase):
        self.near(phase)
        self.far(phase)

    def sent(self, phase):
        for slot in range(6):
            self.copy(phase, slot).wait_send()


def each(rings, *steps):
    for name, phase in steps:
        for ring in rings:
            getattr(ring, name)(phase)


def same_head():
    c = lax.broadcasted_iota(jnp.int32, (PAIR, PAIR), 0) // ATTEND_DIM
    v = lax.broadcasted_iota(jnp.int32, (PAIR, PAIR), 1) // ATTEND_DIM
    return c == v


LEVELS = 7
QUAD = 256


def windows():
    t = lax.broadcasted_iota(jnp.int32, (CHUNK, QUAD), 0)
    s = lax.broadcasted_iota(jnp.int32, (CHUNK, QUAD), 1) % CHUNK
    chosen = [s < t, s > t]
    for level in range(LEVELS):
        middle = (((t >> (level + 1)) << 1) + 1) << level
        late = ((s >= middle) & (s < t)) & (t >= middle)
        early = ((s > t) & (s < middle)) & (t < middle)
        chosen.append(late | early)
    return [jnp.where(c, 1.0, 0.0).astype(bf16) for c in chosen]


def halves(values):
    first_head = lax.broadcasted_iota(jnp.int32, (1, PAIR), 1) < ATTEND_DIM
    return jnp.concatenate(
        [jnp.where(first_head, values, 0.0), jnp.where(first_head, 0.0, values)], axis=0
    ).astype(bf16)


def layer_kernel(
    extents_ref, x_ref, perm_ref, gain_ref, blend_ref, left_ref, w_ref, w_out_ref,
    right_ref, speed_ref, reward_ref, scale_ref,
    out_ref, state_ref, slots0, slots1, slots2,
    slots, stack, mixed, chosen, picked, total, stats, low_rank, lora_ref, last, tail, turned,
    valid_ref, level_of, own_state, own_total, far_state, far_total,
    load_sem, place_sem, tail_sem, send, recv, out_send, out_recv,
    state_send, state_recv, total_send, total_recv, ready, fetch_sem, part_send, part_recv, save_sem,
):
    rows, width = x_ref.shape
    reqs = last.shape[0]
    span = rows // reqs
    at = position()
    half = w_ref.shape[1] // 2
    parts = (slice(0, half), slice(half, 2 * half))
    rings = [
        Ring(slots.at[m], ORDERS[m], PLACES[m], send.at[m], recv.at[m], parts) for m in range(3)
    ]
    load = pltpu.make_async_copy(x_ref, stack.at[pl.ds(0, rows)], load_sem)
    load.start()
    for m in range(3):
        slots[(m, *(at[axis] for axis in PLACES[m]))] = w_ref[m].astype(bf16)
    core = lax.axis_index("tensor")
    partner = (1 - core, lax.axis_index("req"), at["y"])
    far_state[...] = jnp.zeros_like(far_state)
    far_total[...] = jnp.zeros_like(far_total)
    barrier = pltpu.get_barrier_semaphore()
    friends = [device(moved(at, axis, by)) for axis in "xyz" for by in (1, -1)]
    for friend in friends + [device(moved(at, "y", 2)), partner]:
        pl.semaphore_signal(barrier, inc=1, device_id=friend, device_id_type=MESH)
    pl.semaphore_wait(barrier, 8)
    each(rings, ("start", 0))
    load.wait()
    for b in range(reqs):
        end = (b + 1) * span
        last[b : b + 1, :] = stack[end - 16 : end, :].astype(f32)[15:16].astype(bf16)
    tail_on = pltpu.make_async_remote_copy(
        last, tail, tail_sem.at[0], tail_sem.at[1],
        device_id=device(moved(at, "y", 1)), device_id_type=MESH,
    )
    tail_on.start()

    out_slots = (slots0, slots1, slots2)
    out_rings = []
    turned[...] = w_out_ref[...].T.astype(bf16)
    placed = []
    for i in range(3):
        own = out_slots[i].at[at["x"], at["z"], at["y"]]
        cut = turned.at[:, OUT_CUTS[i] : OUT_CUTS[i + 1]]
        placed.append(pltpu.make_async_copy(cut, own, place_sem.at[i]))
        placed[i].start()
        out_rings.append(
            Ring(out_slots[i], ORDERS[i], ("x", "z", "y"), out_send.at[i], out_recv.at[i], parts)
        )

    table = jnp.concatenate([gain_ref[...], blend_ref[0:3, :]], axis=0)
    first = table.astype(bf16)
    rest = table - first.astype(f32)
    second = rest.astype(bf16)
    third = (rest - second.astype(f32)).astype(bf16)
    each(rings, ("turn", 0))
    tail_on.wait_recv()
    before = jnp.where(at["y"] > 0, tail[...].astype(f32), 0.0).astype(bf16)
    pad = jnp.zeros((16 - reqs - 12, width), bf16)
    stack[rows:, :] = jnp.concatenate([before, first, second, third, pad], axis=0)
    low_rank[...] = jnp.zeros_like(low_rank)

    def row_stats(i, _):
        here = pl.ds(pl.multiple_of(i * 16, 16), 16)
        part = stack[here, :].astype(f32)
        mean = jnp.mean(part, axis=-1, keepdims=True)
        centred = part - mean
        spread = jnp.mean(centred * centred, axis=-1, keepdims=True)
        stats[0, here, :] = jnp.broadcast_to(mean, (16, PAIR))
        stats[1, here, :] = jnp.broadcast_to(lax.rsqrt(spread + eps), (16, PAIR))
        return 0

    lax.fori_loop(0, stack.shape[0] // 16, row_stats, 0)
    each(rings, ("settle", 0), ("start", 1))
    for place in placed:
        place.wait()

    def shifted(values, gain):
        mean, scale = stats[0, :, 0:1], stats[1, :, 0:1]
        row = lax.broadcasted_iota(jnp.int32, (rows, 1), 0)
        normal = (values - mean) * scale * gain
        current = normal[:rows]
        previous = pltpu.roll(current, 1, axis=0)
        for b in range(reqs):
            previous = jnp.where(row == b * span, normal[rows + b : rows + b + 1], previous)
        return current, previous - current

    piece = STEP // 2
    depth = chosen.shape[0]

    def mix_step(step, _):
        here = pl.ds(pl.multiple_of(step * STEP, STEP), STEP)
        y, x0 = step // 2, (step % 2) * 2
        names = []
        for i in range(2):
            for z in range(0, SIDE, 2):
                at_row = (x0 + i) * 8 + z * 2 + y // 2
                low, high = perm_ref[pl.ds(at_row, 1), :], perm_ref[pl.ds(at_row + 2, 1), :]
                low_up, high_up = pltpu.roll(low, 64, axis=1), pltpu.roll(high, 64, axis=1)
                even = y % 2 == 0
                names.append(
                    jnp.where(
                        lax.broadcasted_iota(jnp.int32, (1, 128), 1) < 64,
                        jnp.where(even, low, low_up), jnp.where(even, high_up, high),
                    )
                )
        names = jnp.concatenate(names, axis=1)
        picked[...] = jnp.zeros_like(picked)

        def pick(d, _):
            def one_hot(i, _):
                base = pl.multiple_of(i * 128, 128)
                feature = lax.broadcasted_iota(jnp.int32, (128, STEP), 0) + (base + d * depth)
                chosen[pl.ds(base, 128), :] = (feature == names).astype(f32).astype(bf16)
                return 0

            lax.fori_loop(0, depth // 128, one_hot, 0)
            source = stack[:, pl.ds(pl.multiple_of(d * depth, depth), depth)]
            picked[...] += dot32(source, chosen[...])
            return 0

        lax.fori_loop(0, width // depth, pick, 0)
        for i in range(2):
            values = picked[:, i * piece : (i + 1) * piece]
            own = values[rows + reqs :]
            own = own[0:4] + own[4:8] + own[8:12]
            current, delta = shifted(values, own[0:1])
            blended = [(current + delta * own[1 + j : 2 + j]).astype(bf16) for j in range(3)]
            picked[:rows, i * piece : (i + 1) * piece] = blended[0].astype(f32)
            mixed[1, x0 + i, :, pl.ds(pl.multiple_of(y * piece, piece), piece)] = blended[1]
            mixed[2, y, :, pl.ds(pl.multiple_of((x0 + i) * piece, piece), piece)] = blended[2]
        columns = pl.ds(pl.multiple_of(step * 128, 128), 128)
        for z in range(SIDE):
            pair = [picked[:rows, i * piece + z * 64 : i * piece + (z + 1) * 64] for i in range(2)]
            mixed[0, z, :, columns] = jnp.concatenate(pair, axis=1).astype(bf16)

        current, delta = shifted(stack[:, here].astype(f32), gain_ref[:, here])
        low_rank[...] += dot32(
            (current + delta * blend_ref[3:4, here]).astype(bf16),
            left_ref[pl.ds(pl.multiple_of(step * STEP, STEP), STEP), :],
        )

        for when, group, steps in (
            (0, rings, (("turn", 1),)),
            (2, rings, (("settle", 1), ("start", 2))),
            (3, out_rings, (("start", 0),)),
            (4, out_rings, (("turn", 0),)),
            (5, out_rings, (("settle", 0), ("start", 1))),
            (7, out_rings, (("turn", 1),)),
            (7, rings, (("turn", 2),)),
        ):
            @pl.when(step == when)
            def _():
                each(group, *steps)

        return 0

    lax.fori_loop(0, width // STEP, mix_step, 0)
    lora_ref[...] = jnp.tanh(low_rank[...]).astype(bf16)

    def products(offset, fresh):
        def tile(i, _):
            m, n = i // 4, i % 4
            own = jnp.where(m == 0, at["z"], jnp.where(m == 1, at["x"], at["y"]))
            plane = (own + offset) % SIDE
            here = pl.ds(pl.multiple_of(n * 256, 256), 256)
            weight = slots[m, plane, :, :, :, here].reshape(width // SIDE, 256)
            product = dot32(mixed[m, plane], weight)
            if fresh:
                total[m, :, here] = product
            elif offset == 2:
                mixed[m, own, :, here] = (total[m, :, here] + product).astype(bf16)
            else:
                total[m, :, here] += product
            return 0

        lax.fori_loop(0, 12, tile, 0)

    products(0, True)
    each(rings, ("near", 2))
    products(1, False)
    products(3, False)
    each(out_rings, ("settle", 1))
    sums = [(slice(CHUNK * i, CHUNK * (i + 1)), slice(0, QUAD)) for i in range(8)]
    sums.append((slice(0, CHUNK), slice(QUAD, 2 * QUAD)))
    row = lax.broadcasted_iota(jnp.int32, (rows, PAIR), 0)
    token = at["y"] * span + row % span
    inside = jnp.zeros((rows, PAIR), f32)
    for b in range(reqs):
        inside = jnp.where((row // span == b) & (token < extents_ref[b]), 1.0, inside)
    valid_ref[...] = inside

    for i, window in enumerate(windows()):
        chosen[sums[i]] = window
    t = lax.broadcasted_iota(jnp.int32, (CHUNK, QUAD), 0)
    s = lax.broadcasted_iota(jnp.int32, (CHUNK, QUAD), 1) % CHUNK
    level = jnp.full((CHUNK, QUAD), LEVELS, jnp.int32)
    for i in range(LEVELS):
        level = jnp.where(((t >> i) == (s >> i) + 1) & (((t >> i) & 1) == 1), i, level)
    level_of[...] = level
    each(rings, ("far", 2))
    each(out_rings, ("start", 2))
    products(2, False)
    pl.semaphore_signal(ready, inc=1, device_id=partner, device_id_type=MESH)
    def place(m, offset):
        return mixed.at[m, (at[PLACES[m][0]] + offset) % SIDE]

    rkv = [place(m, 0) for m in range(3)]
    faded, normed = place(0, 1), place(0, 3)
    y_buf, decays = total.at[0], total.at[1]
    local_width = total.shape[2]
    share = width // 2

    def tiles(m, offsets):
        planes = [(at[PLACES[m][0]] + offset) % SIDE for offset in offsets]

        def tile(j):
            plane = jnp.where(j < 4, planes[0], planes[1])
            return mixed.at[m, plane, :, pl.ds(pl.multiple_of(j % 4 * QUAD, QUAD), QUAD)]

        return tile

    outgoing, incoming = tiles(1, (1, 2)), tiles(2, (1, 2))
    keep = same_head()
    ones = jnp.where(keep, 1.0, 0.0).astype(bf16)
    head_sum = jnp.concatenate([ones, ones], axis=0)
    first_head = lax.broadcasted_iota(jnp.int32, (1, PAIR), 1) < ATTEND_DIM

    def over_head(values):
        return dot32(jnp.concatenate(split_two(values), axis=1), head_sum)

    def prepare(q, _):
        lanes = pl.ds(pl.multiple_of(q * QUAD, QUAD), QUAD)
        valid = valid_ref[:, 0:1]
        rate = jnp.exp(dot32(lora_ref[...], right_ref[:, lanes]))
        decays[:, lanes] = -speed_ref[:, lanes] * rate * valid
        for b in range(reqs):
            before, after, total = [], [], []
            for c in range(span // CHUNK):
                rows_c = slice(b * span + c * CHUNK, b * span + (c + 1) * CHUNK)
                w = decays[rows_c, lanes]
                both = jnp.concatenate(split_two(w), axis=0)
                before.append(dot32(chosen[sums[0]], both))
                after.append(dot32(chosen[sums[1]], both))
                total.append(before[c][CHUNK - 1 :] + w[CHUNK - 1 :])
            own_total[b : b + 1, lanes] = total[0] + total[1]
            at0 = slice(b * span, b * span + CHUNK)
            at1 = slice(b * span + CHUNK, (b + 1) * span)
            whole = slice(b * span, (b + 1) * span)
            r0, r1 = rkv[0][at0, lanes].astype(f32), rkv[0][at1, lanes].astype(f32)
            k0 = rkv[1][at0, lanes].astype(f32) * valid[at0]
            k1 = rkv[1][at1, lanes].astype(f32) * valid[at1]
            faded[at0, lanes] = (r0 * jnp.exp(before[0])).astype(bf16)
            faded[at1, lanes] = (r1 * jnp.exp(before[1] + total[0])).astype(bf16)
            query1 = (r1 * jnp.exp(before[1])).astype(bf16)
            key0 = (k0 * jnp.exp(after[0])).astype(bf16)
            keys = jnp.concatenate(
                [(k0 * jnp.exp(after[0] + total[1])).astype(bf16), (k1 * jnp.exp(after[1])).astype(bf16)],
                axis=0,
            )
            value = rkv[2][whole, lanes]
            bonus0 = r0 * k0 * reward_ref[:, lanes]
            bonus1 = r1 * k1 * reward_ref[:, lanes]
            for p in range(2):
                pair = slice(p * PAIR, (p + 1) * PAIR)
                here = pl.ds(pl.multiple_of(q * QUAD + p * PAIR, PAIR), PAIR)
                grown = dot32(value[:, pair], keys[:, pair], CONTRACT_ROWS)
                own_state[b, 2 * q + p] = jnp.where(
                    first_head, grown[:ATTEND_DIM], grown[ATTEND_DIM:]
                ).astype(bf16)
                grown0 = dot32(value[:CHUNK, pair], key0[:, pair], CONTRACT_ROWS)
                grown0 = jnp.where(keep, grown0, 0.0).astype(bf16)
                y_buf[at0, here] = over_head(bonus0[:, pair]) * value[:CHUNK, pair].astype(f32)
                y_buf[at1, here] = over_head(bonus1[:, pair]) * value[CHUNK:, pair].astype(
                    f32
                ) + dot32(query1[:, pair], grown0, CONTRACT_LANES)

        return 0

    lax.fori_loop(0, local_width // QUAD, prepare, 0)

    def hand_on(by):
        to = device(moved(at, "y", by))
        return [
            pltpu.make_async_remote_copy(
                own, far.at[by - 1], s_sem.at[by - 1], r_sem.at[by - 1],
                device_id=to, device_id_type=MESH,
            )
            for own, far, s_sem, r_sem in (
                (own_state, far_state, state_send, state_recv),
                (own_total, far_total, total_send, total_recv),
            )
        ]

    for by in range(1, SIDE):
        @pl.when(at["y"] + by < SIDE)
        def _():
            for copy in hand_on(by):
                copy.start()

    def expo(n, p=None):
        first = n % 2 * QUAD + (0 if p is None else p * PAIR)
        lanes = slice(first, first + (QUAD if p is None else PAIR))
        return slice(n // 2 * CHUNK, (n // 2 + 1) * CHUNK), lanes

    def within(i, _):
        q, c = i // 4, i % 4
        lanes = pl.ds(pl.multiple_of(q * QUAD, QUAD), QUAD)
        rows_c = pl.ds(pl.multiple_of(c * CHUNK, CHUNK), CHUNK)
        both = jnp.concatenate(split_two(decays[rows_c, lanes]), axis=0)
        for n in range(LEVELS):
            picked[expo(n)] = dot32(chosen[sums[2 + n]], both)
        row = lax.broadcasted_iota(jnp.int32, (CHUNK, 1), 0)
        valid = valid_ref[rows_c, 0:1]
        for p in range(2):
            pair = slice(p * PAIR, (p + 1) * PAIR)
            here = pl.ds(pl.multiple_of(q * QUAD + p * PAIR, PAIR), PAIR)
            r = rkv[0][rows_c, here].astype(f32)
            k = rkv[1][rows_c, here].astype(f32) * valid
            scores = jnp.zeros((CHUNK, QUAD), f32)
            for n in range(LEVELS):
                side = jnp.where(((row >> n) & 1) == 1, r, k) * jnp.exp(picked[expo(n, p)])
                found = dot32(side.astype(bf16), halves(side), CONTRACT_LANES)
                scores = jnp.where(level_of[...] == n, found, scores)
            values = halves(rkv[2][rows_c, here].astype(f32))
            y_buf[rows_c, here] += dot32(scores.astype(bf16), values)

        @pl.when(i == 3)
        def _():
            each(out_rings, ("turn", 2))

        return 0

    lax.fori_loop(0, local_width // QUAD * (rows // CHUNK), within, 0)

    for by in range(1, SIDE):
        @pl.when(at["y"] >= by)
        def _():
            for copy in hand_on(by):
                copy.wait_recv()

    def finish(p, _):
        here = pl.ds(pl.multiple_of(p * PAIR, PAIR), PAIR)
        for b in range(reqs):
            whole = slice(b * span, (b + 1) * span)
            near = far_total[0, b : b + 1, here]
            state = (
                far_state[0, b, p].astype(f32)
                + jnp.exp(near) * far_state[1, b, p].astype(f32)
                + jnp.exp(near + far_total[1, b : b + 1, here]) * far_state[2, b, p].astype(f32)
            )
            final = jnp.exp(own_total[b : b + 1, here]) * state + own_state[b, p].astype(f32)
            state_ref[b, p] = final.T
            y = y_buf[whole, here] + dot32(faded[whole, here], halves(state), CONTRACT_LANES)
            centred = y - over_head(y) * (1.0 / ATTEND_DIM)
            spread = over_head(centred * centred) * (1.0 / ATTEND_DIM)
            scaled = centred * lax.rsqrt(spread + eps) * scale_ref[:, here]
            normed[whole, here] = (scaled * valid_ref[whole, 0:1]).astype(bf16)
        return 0

    lax.fori_loop(0, local_width // PAIR, finish, 0)
    each(out_rings, ("settle", 2))

    def fetch(t):
        x, z = 2 * jnp.where(t < 8, 1 - core, core) + t % 8 // SIDE, t % SIDE
        return [
            pltpu.make_async_copy(
                out_slots[i].at[x, z],
                slots.at[0, x, z, :, :, OUT_CUTS[i] : OUT_CUTS[i + 1]],
                fetch_sem.at[t, i],
            )
            for i in range(3)
        ]

    def begin(t, _):
        for copy in fetch(t):
            copy.start()
        return 0

    each(rings, ("sent", 0), ("sent", 1), ("sent", 2))
    lax.fori_loop(0, 16, begin, 0)

    def terms(t):
        for copy in fetch(t):
            copy.wait()
        weight = slots[0, 2 * jnp.where(t < 8, 1 - core, core) + t % 8 // SIDE, t % SIDE]
        weight = weight.reshape(QUAD, local_width)
        return dot32(normed[...], weight, CONTRACT_LANES).astype(bf16)

    def exchange(j):
        return pltpu.make_async_remote_copy(
            outgoing(j), incoming(j), part_send.at[j], part_recv.at[j],
            device_id=partner, device_id_type=MESH,
        )

    pl.semaphore_wait(ready, 1)

    def give(j, _):
        outgoing(j)[...] = terms(j)
        exchange(j).start()
        return 0

    lax.fori_loop(0, 8, give, 0)

    def save(j):
        here = pl.ds(pl.multiple_of(j * QUAD, QUAD), QUAD)
        return pltpu.make_async_copy(incoming(j), out_ref.at[:, here], save_sem.at[j])

    def keep_own(j, _):
        here = pl.ds(pl.multiple_of(core * share + j * QUAD, QUAD), QUAD)
        mine = terms(j + 8).astype(f32)
        exchange(j).wait_recv()
        summed = mine + incoming(j)[...].astype(f32)
        incoming(j)[...] = (stack[:rows, here].astype(f32) + summed).astype(bf16)
        save(j).start()
        return 0

    lax.fori_loop(0, 8, keep_own, 0)

    def ended(j, _):
        exchange(j).wait_send()
        save(j).wait()
        return 0

    lax.fori_loop(0, 8, ended, 0)
    for by in range(1, SIDE):
        @pl.when(at["y"] + by < SIDE)
        def _():
            for copy in hand_on(by):
                copy.wait_send()
    tail_on.wait_send()
    each(out_rings, ("sent", 0), ("sent", 1), ("sent", 2))


def layer(extents, x, perm, gain, blend, left, weights, out_weight, right, speed, reward, scale):
    rows, width = x.shape
    shard, local_width = weights.shape[1:]
    reqs, inner, pairs = extents.shape[0], left.shape[1], local_width // PAIR
    cuts = [OUT_CUTS[i + 1] - OUT_CUTS[i] for i in range(3)]
    dma = pltpu.SemaphoreType.DMA
    vmem = pl.BlockSpec(memory_space=pltpu.VMEM)
    away = pl.BlockSpec(memory_space=pl.ANY)
    hidden, final, *_ = pl.pallas_call(
        layer_kernel,
        in_specs=[pl.BlockSpec(memory_space=pltpu.SMEM), away] + [vmem] * 10,
        out_specs=[away, vmem, away, away, away],
        out_shape=[
            jax.ShapeDtypeStruct((rows, width // 2), bf16),
            jax.ShapeDtypeStruct((reqs, pairs, PAIR, ATTEND_DIM), f32),
            *(jax.ShapeDtypeStruct((SIDE, SIDE, SIDE, shard, cut), bf16) for cut in cuts),
        ],
        scratch_shapes=[
            pltpu.VMEM((3, SIDE, SIDE, SIDE, shard, local_width), bf16),
            pltpu.VMEM((rows + 16, width), bf16),
            pltpu.VMEM((3, SIDE, rows, width // SIDE), bf16),
            pltpu.VMEM((width // 4, STEP), bf16),
            pltpu.VMEM((rows + 16, STEP), f32),
            pltpu.VMEM((3, rows, local_width), f32),
            pltpu.VMEM((2, rows + 16, PAIR), f32),
            pltpu.VMEM((rows, inner), f32),
            pltpu.VMEM((rows, inner), bf16),
            pltpu.VMEM((reqs, width), bf16),
            pltpu.VMEM((reqs, width), bf16),
            pltpu.VMEM((shard, local_width), bf16),
            pltpu.VMEM((rows, PAIR), f32),
            pltpu.VMEM((CHUNK, QUAD), jnp.int32),
            pltpu.VMEM((reqs, pairs, ATTEND_DIM, PAIR), bf16),
            pltpu.VMEM((reqs, local_width), f32),
            pltpu.VMEM((3, reqs, pairs, ATTEND_DIM, PAIR), bf16),
            pltpu.VMEM((3, reqs, local_width), f32),
            dma, dma((3,)), dma((2,)),
            dma((3, 3, 6)), dma((3, 3, 6)), dma((3, 3, 6)), dma((3, 3, 6)),
            dma((3,)), dma((3,)), dma((3,)), dma((3,)),
            pltpu.SemaphoreType.REGULAR, dma((16, 3)), dma((8,)), dma((8,)), dma((8,)),
        ],
        compiler_params=pltpu.CompilerParams(
            collective_id=0, has_side_effects=True, vmem_limit_bytes=61 << 20
        ),
        cost_estimate=pl.CostEstimate(
            flops=100 * 10**9, bytes_accessed=64 << 20, transcendentals=0
        ),
        name="layer",
    )(extents, x, perm, gain, blend, left, weights, out_weight, right, speed, reward, scale)
    return hidden, final


def local(
    incoming_activations,
    standardize_scaling,
    lagged_blending_weights,
    learner_line_permutation,
    learner_acceptor_lookup_slices,
    learner_projection_slices,
    fading_left_matrix,
    fading_right_matrix,
    feature_fading_speed,
    self_reward,
    cluster_scaling_vector,
    prompt_extents,
):
    reqs, span, width = incoming_activations.shape
    rows = reqs * span
    local_width = feature_fading_speed.shape[0]
    x = incoming_activations.reshape(rows, width)
    hidden, final = layer(
        prompt_extents, x, learner_line_permutation.reshape(width // PAIR, PAIR),
        standardize_scaling[None], lagged_blending_weights, fading_left_matrix,
        learner_acceptor_lookup_slices, learner_projection_slices, fading_right_matrix,
        feature_fading_speed[None], self_reward[None], cluster_scaling_vector[None],
    )
    stretch_states = final.reshape(reqs, 1, local_width // ATTEND_DIM, ATTEND_DIM * ATTEND_DIM)
    return (hidden.reshape(reqs, span, hidden.shape[1]), stretch_states)


def solution(mesh):
    in_specs = (
        P("req", "seq", None),
        P(),
        P(),
        P(),
        P(None, ("req", "seq"), "tensor"),
        P("tensor", ("req", "seq")),
        P(),
        P(None, "tensor"),
        P("tensor"),
        P("tensor"),
        P("tensor"),
        P("req"),
    )
    out_specs = (P("req", "seq", "tensor"), P("req", "seq", "tensor", None))
    return jax.shard_map(local, mesh=mesh, in_specs=in_specs, out_specs=out_specs, check_vma=False)
```

```python
import functools

import jax
import jax.numpy as jnp
from jax import lax
from jax.experimental import pallas as pl
from jax.experimental.pallas import tpu as pltpu
from jax.sharding import PartitionSpec as P

ATTEND_DIM = 64
PAIR = 128
CHUNK = 128
eps = 1e-05
f32 = jnp.float32
bf16 = jnp.bfloat16
CONTRACT_ROWS = (((0,), (0,)), ((), ()))
CONTRACT_LANES = (((1,), (1,)), ((), ()))


def split_two(value):
    high = value.astype(bf16)
    low = (value - high.astype(f32)).astype(bf16)
    return high, low


def dot32(a, b, dims=(((1,), (0,)), ((), ()))):
    return lax.dot_general(a, b, dims, preferred_element_type=f32)


MESH = pl.DeviceIdType.MESH
ORDERS = (("x", "y", "z"), ("y", "z", "x"), ("z", "x", "y"))
PLACES = (("z", "y", "x"), ("x", "y", "z"), ("y", "x", "z"))
SIDE = 4
STEP = 512
OUT_CUTS = (0, 384, 768, 1024)


def position():
    req = lax.axis_index("req")
    return {"x": req // SIDE, "z": req % SIDE, "y": lax.axis_index("seq")}


def moved(at, axis, by):
    return {**at, axis: (at[axis] + by + SIDE) % SIDE}


def device(at):
    return (lax.axis_index("tensor"), at["x"] * SIDE + at["z"], at["y"])


class Ring:
    def __init__(self, slots, order, places, send, recv, parts):
        self.slots, self.order, self.places = slots, order, places
        self.send, self.recv, self.parts = send, recv, parts
        self.at = position()

    def block(self, phase, where, part):
        index = []
        for axis in self.places:
            turn = self.order.index(axis)
            index.append(slice(None) if turn < phase else where if turn == phase else self.at[axis])
        return self.slots.at[(*index, *part)]

    def copy(self, phase, slot):
        axis = self.order[phase]
        right = slot in (0, 2, 4)
        part = 0 if slot in (0, 3, 4) else 1
        by = 1 if right else -1
        source = self.at if slot < 4 else moved(self.at, axis, -by)
        ref = self.block(phase, source[axis], (self.parts[part],))
        return pltpu.make_async_remote_copy(
            ref, ref, self.send.at[phase, slot], self.recv.at[phase, slot],
            device_id=device(moved(self.at, axis, by)), device_id_type=MESH,
        )

    def start(self, phase):
        for slot in range(4):
            self.copy(phase, slot).start()

    def turn(self, phase):
        for slot in range(2):
            self.copy(phase, slot).wait_recv()
            self.copy(phase, slot + 4).start()

    def near(self, phase):
        for slot in range(2, 4):
            self.copy(phase, slot).wait_recv()

    def far(self, phase):
        for slot in range(4, 6):
            self.copy(phase, slot).wait_recv()

    def settle(self, phase):
        self.near(phase)
        self.far(phase)

    def own_sent(self, phase):
        for slot in range(4):
            self.copy(phase, slot).wait_send()

    def passed_on(self, phase):
        for slot in range(4, 6):
            self.copy(phase, slot).wait_send()

    def sent(self, phase):
        self.own_sent(phase)
        self.passed_on(phase)


def each(rings, *steps):
    for name, phase in steps:
        for ring in rings:
            getattr(ring, name)(phase)


def same_head():
    c = lax.broadcasted_iota(jnp.int32, (PAIR, PAIR), 0) // ATTEND_DIM
    v = lax.broadcasted_iota(jnp.int32, (PAIR, PAIR), 1) // ATTEND_DIM
    return c == v


LEVELS = 7
QUAD = 256


def windows():
    t = lax.broadcasted_iota(jnp.int32, (CHUNK, QUAD), 0)
    s = lax.broadcasted_iota(jnp.int32, (CHUNK, QUAD), 1) % CHUNK
    chosen = [s < t, s > t]
    for level in range(LEVELS):
        middle = (((t >> (level + 1)) << 1) + 1) << level
        late = ((s >= middle) & (s < t)) & (t >= middle)
        early = ((s > t) & (s < middle)) & (t < middle)
        chosen.append(late | early)
    return [jnp.where(c, 1.0, 0.0).astype(bf16) for c in chosen]


def halves(values):
    first_head = lax.broadcasted_iota(jnp.int32, (1, PAIR), 1) < ATTEND_DIM
    return jnp.concatenate(
        [jnp.where(first_head, values, 0.0), jnp.where(first_head, 0.0, values)], axis=0
    ).astype(bf16)


def layer_kernel(
    extents_ref, x_ref, perm_ref, gain_ref, blend_ref, left_ref, w_ref, w_out_ref,
    right_ref, speed_ref, reward_ref, scale_ref,
    out_ref, state_ref, slots0, slots1, slots2,
    slots, stack, mixed, chosen, picked, total, stats, low_rank, lora_ref, last, tail, turned,
    valid_ref, level_of, own_state, own_total, far_state, far_total,
    load_sem, place_sem, tail_sem, send, recv, out_send, out_recv,
    state_send, state_recv, total_send, total_recv, ready, fetch_sem, part_send, part_recv, save_sem,
):
    rows, width = x_ref.shape
    reqs = last.shape[0]
    span = rows // reqs
    at = position()
    half = w_ref.shape[1] // 2
    parts = (slice(0, half), slice(half, 2 * half))
    rings = [
        Ring(slots.at[m], ORDERS[m], PLACES[m], send.at[m], recv.at[m], parts) for m in range(3)
    ]
    load = pltpu.make_async_copy(x_ref, stack.at[pl.ds(0, rows)], load_sem)
    load.start()
    for m in range(3):
        slots[(m, *(at[axis] for axis in PLACES[m]))] = w_ref[m].astype(bf16)
    core = lax.axis_index("tensor")
    partner = (1 - core, lax.axis_index("req"), at["y"])
    far_state[...] = jnp.zeros_like(far_state)
    far_total[...] = jnp.zeros_like(far_total)
    barrier = pltpu.get_barrier_semaphore()
    friends = [device(moved(at, axis, by)) for axis in "xyz" for by in (1, -1)]
    for friend in friends + [device(moved(at, "y", 2)), partner]:
        pl.semaphore_signal(barrier, inc=1, device_id=friend, device_id_type=MESH)
    pl.semaphore_wait(barrier, 8)
    each(rings, ("start", 0))
    load.wait()
    for b in range(reqs):
        end = (b + 1) * span
        last[b : b + 1, :] = stack[end - 16 : end, :].astype(f32)[15:16].astype(bf16)
    tail_on = pltpu.make_async_remote_copy(
        last, tail, tail_sem.at[0], tail_sem.at[1],
        device_id=device(moved(at, "y", 1)), device_id_type=MESH,
    )
    tail_on.start()

    out_slots = (slots0, slots1, slots2)
    out_rings = []
    turned[...] = w_out_ref[...].astype(bf16)
    placed = []
    for i in range(3):
        own = out_slots[i].at[at["x"], at["z"], at["y"]]
        cut = turned.at[:, OUT_CUTS[i] : OUT_CUTS[i + 1]]
        placed.append(pltpu.make_async_copy(cut, own, place_sem.at[i]))
        placed[i].start()
        out_rings.append(
            Ring(out_slots[i], ORDERS[i], ("x", "z", "y"), out_send.at[i], out_recv.at[i], parts)
        )

    table = jnp.concatenate([gain_ref[...], blend_ref[0:3, :]], axis=0)
    first = table.astype(bf16)
    rest = table - first.astype(f32)
    second = rest.astype(bf16)
    third = (rest - second.astype(f32)).astype(bf16)
    each(rings, ("turn", 0))
    tail_on.wait_recv()
    before = jnp.where(at["y"] > 0, tail[...].astype(f32), 0.0).astype(bf16)
    pad = jnp.zeros((16 - reqs - 12, width), bf16)
    stack[rows:, :] = jnp.concatenate([before, first, second, third, pad], axis=0)
    low_rank[...] = jnp.zeros_like(low_rank)

    def row_stats(i, _):
        here = pl.ds(pl.multiple_of(i * 16, 16), 16)
        part = stack[here, :].astype(f32)
        mean = jnp.mean(part, axis=-1, keepdims=True)
        centred = part - mean
        spread = jnp.mean(centred * centred, axis=-1, keepdims=True)
        stats[0, here, :] = jnp.broadcast_to(mean, (16, PAIR))
        stats[1, here, :] = jnp.broadcast_to(lax.rsqrt(spread + eps), (16, PAIR))
        return 0

    lax.fori_loop(0, stack.shape[0] // 16, row_stats, 0)
    each(rings, ("settle", 0), ("start", 1))
    for place in placed:
        place.wait()

    def shifted(values, gain):
        mean, scale = stats[0, :, 0:1], stats[1, :, 0:1]
        row = lax.broadcasted_iota(jnp.int32, (rows, 1), 0)
        normal = (values - mean) * scale * gain
        current = normal[:rows]
        previous = pltpu.roll(current, 1, axis=0)
        for b in range(reqs):
            previous = jnp.where(row == b * span, normal[rows + b : rows + b + 1], previous)
        return current, previous - current

    piece = STEP // 2
    depth = chosen.shape[0]

    def mix_step(step, _):
        here = pl.ds(pl.multiple_of(step * STEP, STEP), STEP)
        y, x0 = step // 2, (step % 2) * 2
        names = []
        for i in range(2):
            for z in range(0, SIDE, 2):
                at_row = (x0 + i) * 8 + z * 2 + y // 2
                low, high = perm_ref[pl.ds(at_row, 1), :], perm_ref[pl.ds(at_row + 2, 1), :]
                low_up, high_up = pltpu.roll(low, 64, axis=1), pltpu.roll(high, 64, axis=1)
                even = y % 2 == 0
                names.append(
                    jnp.where(
                        lax.broadcasted_iota(jnp.int32, (1, 128), 1) < 64,
                        jnp.where(even, low, low_up), jnp.where(even, high_up, high),
                    )
                )
        names = jnp.concatenate(names, axis=1)
        picked[...] = jnp.zeros_like(picked)

        def pick(d, _):
            def one_hot(i, _):
                base = pl.multiple_of(i * 128, 128)
                feature = lax.broadcasted_iota(jnp.int32, (128, STEP), 0) + (base + d * depth)
                chosen[pl.ds(base, 128), :] = (feature == names).astype(f32).astype(bf16)
                return 0

            lax.fori_loop(0, depth // 128, one_hot, 0)
            source = stack[:, pl.ds(pl.multiple_of(d * depth, depth), depth)]
            picked[...] += dot32(source, chosen[...])
            return 0

        lax.fori_loop(0, width // depth, pick, 0)
        for i in range(2):
            values = picked[:, i * piece : (i + 1) * piece]
            own = values[rows + reqs :]
            own = own[0:4] + own[4:8] + own[8:12]
            current, delta = shifted(values, own[0:1])
            blended = [(current + delta * own[1 + j : 2 + j]).astype(bf16) for j in range(3)]
            picked[:rows, i * piece : (i + 1) * piece] = blended[0].astype(f32)
            mixed[1, x0 + i, :, pl.ds(pl.multiple_of(y * piece, piece), piece)] = blended[1]
            mixed[2, y, :, pl.ds(pl.multiple_of((x0 + i) * piece, piece), piece)] = blended[2]
        columns = pl.ds(pl.multiple_of(step * 128, 128), 128)
        for z in range(SIDE):
            pair = [picked[:rows, i * piece + z * 64 : i * piece + (z + 1) * 64] for i in range(2)]
            mixed[0, z, :, columns] = jnp.concatenate(pair, axis=1).astype(bf16)

        current, delta = shifted(stack[:, here].astype(f32), gain_ref[:, here])
        low_rank[...] += dot32(
            (current + delta * blend_ref[3:4, here]).astype(bf16),
            left_ref[pl.ds(pl.multiple_of(step * STEP, STEP), STEP), :],
        )

        for when, group, steps in (
            (0, rings, (("turn", 1),)),
            (2, rings, (("settle", 1), ("start", 2))),
            (3, out_rings, (("start", 0),)),
            (4, out_rings, (("turn", 0),)),
            (5, out_rings, (("settle", 0), ("start", 1))),
            (7, out_rings, (("turn", 1),)),
            (7, rings, (("turn", 2),)),
        ):
            @pl.when(step == when)
            def _():
                each(group, *steps)

        return 0

    lax.fori_loop(0, width // STEP, mix_step, 0)
    lora_ref[...] = jnp.tanh(low_rank[...]).astype(bf16)

    def products(offset, fresh):
        def tile(i, _):
            m, n = i // 4, i % 4
            own = jnp.where(m == 0, at["z"], jnp.where(m == 1, at["x"], at["y"]))
            plane = (own + offset) % SIDE
            here = pl.ds(pl.multiple_of(n * 256, 256), 256)
            weight = slots[m, plane, :, :, :, here].reshape(width // SIDE, 256)
            product = dot32(mixed[m, plane], weight)
            if fresh:
                total[m, :, here] = product
            elif offset == 2:
                mixed[m, own, :, here] = (total[m, :, here] + product).astype(bf16)
            else:
                total[m, :, here] += product
            return 0

        lax.fori_loop(0, 12, tile, 0)

    products(0, True)
    each(rings, ("near", 2))
    products(1, False)
    products(3, False)
    each(out_rings, ("settle", 1))
    sums = [(slice(CHUNK * i, CHUNK * (i + 1)), slice(0, QUAD)) for i in range(8)]
    sums.append((slice(0, CHUNK), slice(QUAD, 2 * QUAD)))
    row = lax.broadcasted_iota(jnp.int32, (rows, PAIR), 0)
    token = at["y"] * span + row % span
    inside = jnp.zeros((rows, PAIR), f32)
    for b in range(reqs):
        inside = jnp.where((row // span == b) & (token < extents_ref[b]), 1.0, inside)
    valid_ref[...] = inside

    for i, window in enumerate(windows()):
        chosen[sums[i]] = window
    t = lax.broadcasted_iota(jnp.int32, (CHUNK, QUAD), 0)
    s = lax.broadcasted_iota(jnp.int32, (CHUNK, QUAD), 1) % CHUNK
    level = jnp.full((CHUNK, QUAD), LEVELS, jnp.int32)
    for i in range(LEVELS):
        level = jnp.where(((t >> i) == (s >> i) + 1) & (((t >> i) & 1) == 1), i, level)
    level_of[...] = level
    local_width = total.shape[2]

    def place(m, offset):
        return mixed.at[m, (at[PLACES[m][0]] + offset) % SIDE]

    high_decay, low_decay = place(1, 3), place(2, 3)

    def decay(q, _):
        lanes = pl.ds(pl.multiple_of(q * QUAD, QUAD), QUAD)
        rate = jnp.exp(dot32(lora_ref[...], right_ref[:, lanes]))
        high, low = split_two(-speed_ref[:, lanes] * rate * valid_ref[:, 0:1])
        high_decay[:, lanes], low_decay[:, lanes] = high, low
        return 0

    lax.fori_loop(0, local_width // QUAD, decay, 0)

    def split_decay(rows_c, lanes):
        return jnp.concatenate([high_decay[rows_c, lanes], low_decay[rows_c, lanes]], axis=0)

    each(rings, ("sent", 0), ("sent", 1), ("own_sent", 2))

    def level_decay(n, c, lanes):
        m, part = (n - 1) // 2, (n - 1) % 2
        return (
            m, at[PLACES[m][0]], 2 * part + c // 2, pl.ds(c % 2 * 2, 2), slice(None), lanes
        )

    def fade(i, _):
        q, c = i // 4, i % 4
        lanes = pl.ds(pl.multiple_of(q * QUAD, QUAD), QUAD)
        both = split_decay(pl.ds(pl.multiple_of(c * CHUNK, CHUNK), CHUNK), lanes)
        for n in range(1, LEVELS):
            faint = jnp.exp(dot32(chosen[sums[2 + n]], both)).astype(bf16)
            slots[level_decay(n, c, lanes)] = faint.reshape(2, CHUNK // 2, QUAD)
        return 0

    lax.fori_loop(0, local_width // QUAD * (rows // CHUNK), fade, 0)
    each(rings, ("far", 2))
    each(out_rings, ("start", 2))
    products(2, False)
    pl.semaphore_signal(ready, inc=1, device_id=partner, device_id_type=MESH)
    rkv = [place(m, 0) for m in range(3)]
    faded, normed = place(0, 1), place(0, 3)
    y_buf = total.at[0]
    share = width // 2

    def tiles(m, offsets):
        planes = [(at[PLACES[m][0]] + offset) % SIDE for offset in offsets]

        def tile(j):
            plane = jnp.where(j < 4, planes[0], planes[1])
            return mixed.at[m, plane, :, pl.ds(pl.multiple_of(j % 4 * QUAD, QUAD), QUAD)]

        return tile

    outgoing, incoming = tiles(1, (1, 2)), tiles(2, (1, 2))
    keep = same_head()
    ones = jnp.where(keep, 1.0, 0.0).astype(bf16)
    head_sum = jnp.concatenate([ones, ones], axis=0)
    first_head = lax.broadcasted_iota(jnp.int32, (1, PAIR), 1) < ATTEND_DIM

    def over_head(values):
        return dot32(jnp.concatenate(split_two(values), axis=1), head_sum)

    def prepare(q, _):
        lanes = pl.ds(pl.multiple_of(q * QUAD, QUAD), QUAD)
        valid = valid_ref[:, 0:1]
        for b in range(reqs):
            before, after, total = [], [], []
            for c in range(span // CHUNK):
                rows_c = slice(b * span + c * CHUNK, b * span + (c + 1) * CHUNK)
                both = split_decay(rows_c, lanes)
                w = both[:CHUNK].astype(f32) + both[CHUNK:].astype(f32)
                before.append(dot32(chosen[sums[0]], both))
                after.append(dot32(chosen[sums[1]], both))
                total.append(before[c][CHUNK - 1 :] + w[CHUNK - 1 :])
            own_total[b : b + 1, lanes] = total[0] + total[1]
            at0 = slice(b * span, b * span + CHUNK)
            at1 = slice(b * span + CHUNK, (b + 1) * span)
            whole = slice(b * span, (b + 1) * span)
            r0, r1 = rkv[0][at0, lanes].astype(f32), rkv[0][at1, lanes].astype(f32)
            k0 = rkv[1][at0, lanes].astype(f32) * valid[at0]
            k1 = rkv[1][at1, lanes].astype(f32) * valid[at1]
            faded[at0, lanes] = (r0 * jnp.exp(before[0])).astype(bf16)
            faded[at1, lanes] = (r1 * jnp.exp(before[1] + total[0])).astype(bf16)
            query1 = (r1 * jnp.exp(before[1])).astype(bf16)
            key0 = (k0 * jnp.exp(after[0])).astype(bf16)
            keys = jnp.concatenate(
                [(k0 * jnp.exp(after[0] + total[1])).astype(bf16), (k1 * jnp.exp(after[1])).astype(bf16)],
                axis=0,
            )
            value = rkv[2][whole, lanes]
            bonus0 = r0 * k0 * reward_ref[:, lanes]
            bonus1 = r1 * k1 * reward_ref[:, lanes]
            for p in range(2):
                pair = slice(p * PAIR, (p + 1) * PAIR)
                here = pl.ds(pl.multiple_of(q * QUAD + p * PAIR, PAIR), PAIR)
                grown = dot32(value[:, pair], keys[:, pair], CONTRACT_ROWS)
                own_state[b, 2 * q + p] = jnp.where(
                    first_head, grown[:ATTEND_DIM], grown[ATTEND_DIM:]
                ).astype(bf16)
                grown0 = dot32(value[:CHUNK, pair], key0[:, pair], CONTRACT_ROWS)
                grown0 = jnp.where(keep, grown0, 0.0).astype(bf16)
                y_buf[at0, here] = over_head(bonus0[:, pair]) * value[:CHUNK, pair].astype(f32)
                y_buf[at1, here] = over_head(bonus1[:, pair]) * value[CHUNK:, pair].astype(
                    f32
                ) + dot32(query1[:, pair], grown0, CONTRACT_LANES)

        return 0

    lax.fori_loop(0, local_width // QUAD, prepare, 0)

    def hand_on(by):
        to = device(moved(at, "y", by))
        return [
            pltpu.make_async_remote_copy(
                own, far.at[by - 1], s_sem.at[by - 1], r_sem.at[by - 1],
                device_id=to, device_id_type=MESH,
            )
            for own, far, s_sem, r_sem in (
                (own_state, far_state, state_send, state_recv),
                (own_total, far_total, total_send, total_recv),
            )
        ]

    for by in range(1, SIDE):
        @pl.when(at["y"] + by < SIDE)
        def _():
            for copy in hand_on(by):
                copy.start()

    def within(i, _):
        q, c = i // 4, i % 4
        rows_c = pl.ds(pl.multiple_of(c * CHUNK, CHUNK), CHUNK)
        row = lax.broadcasted_iota(jnp.int32, (CHUNK, 1), 0)
        valid = valid_ref[rows_c, 0:1]
        for p in range(2):
            pair = slice(p * PAIR, (p + 1) * PAIR)
            here = pl.ds(pl.multiple_of(q * QUAD + p * PAIR, PAIR), PAIR)
            r = rkv[0][rows_c, here].astype(f32)
            k = rkv[1][rows_c, here].astype(f32) * valid
            scores = jnp.zeros((CHUNK, QUAD), f32)
            for n in range(LEVELS):
                side = jnp.where(((row >> n) & 1) == 1, r, k)
                if n > 0:
                    side = side * slots[level_decay(n, c, here)].reshape(CHUNK, PAIR).astype(f32)
                found = dot32(side.astype(bf16), halves(side), CONTRACT_LANES)
                scores = jnp.where(level_of[...] == n, found, scores)
            values = halves(rkv[2][rows_c, here].astype(f32))
            y_buf[rows_c, here] += dot32(scores.astype(bf16), values)

        @pl.when(i == 3)
        def _():
            each(out_rings, ("turn", 2))

        return 0

    lax.fori_loop(0, local_width // QUAD * (rows // CHUNK), within, 0)

    def fetch(i, offset):
        axis = ORDERS[i][2]
        index = [slice(None)] * 3
        index["xzy".index(axis)] = (at[axis] + offset) % SIDE
        cut = slice(OUT_CUTS[i], OUT_CUTS[i + 1])
        return pltpu.make_async_copy(
            out_slots[i].at[tuple(index)], slots.at[(0, *index, slice(None), cut)],
            fetch_sem.at[i, offset],
        )

    each(rings, ("passed_on", 2))
    each(out_rings, ("near", 2))
    for i in range(3):
        for offset in (0, 1, 3):
            fetch(i, offset).start()
    for by in range(1, SIDE):
        @pl.when(at["y"] >= by)
        def _():
            for copy in hand_on(by):
                copy.wait_recv()

    def finish(p, _):
        here = pl.ds(pl.multiple_of(p * PAIR, PAIR), PAIR)
        for b in range(reqs):
            whole = slice(b * span, (b + 1) * span)
            near = far_total[0, b : b + 1, here]
            state = (
                far_state[0, b, p].astype(f32)
                + jnp.exp(near) * far_state[1, b, p].astype(f32)
                + jnp.exp(near + far_total[1, b : b + 1, here]) * far_state[2, b, p].astype(f32)
            )
            final = jnp.exp(own_total[b : b + 1, here]) * state + own_state[b, p].astype(f32)
            state_ref[b, p] = final.T
            y = y_buf[whole, here] + dot32(faded[whole, here], halves(state), CONTRACT_LANES)
            centred = y - over_head(y) * (1.0 / ATTEND_DIM)
            spread = over_head(centred * centred) * (1.0 / ATTEND_DIM)
            scaled = centred * lax.rsqrt(spread + eps) * scale_ref[:, here]
            normed[whole, here] = (scaled * valid_ref[whole, 0:1]).astype(bf16)
        return 0

    lax.fori_loop(0, local_width // PAIR, finish, 0)
    each(out_rings, ("far", 2))
    for i in range(3):
        fetch(i, 2).start()
    for i in range(3):
        for offset in range(SIDE):
            fetch(i, offset).wait()

    def terms(t):
        weight = slots[0, 2 * jnp.where(t < 8, 1 - core, core) + t % 8 // SIDE, t % SIDE]
        weight = weight.reshape(QUAD, local_width)
        return dot32(normed[...], weight, CONTRACT_LANES).astype(bf16)

    def exchange(j):
        return pltpu.make_async_remote_copy(
            outgoing(j), incoming(j), part_send.at[j], part_recv.at[j],
            device_id=partner, device_id_type=MESH,
        )

    pl.semaphore_wait(ready, 1)

    def give(j, _):
        outgoing(j)[...] = terms(j)
        exchange(j).start()
        return 0

    lax.fori_loop(0, 8, give, 0)

    def save(j):
        here = pl.ds(pl.multiple_of(j * QUAD, QUAD), QUAD)
        return pltpu.make_async_copy(incoming(j), out_ref.at[:, here], save_sem.at[j])

    def keep_own(j, _):
        here = pl.ds(pl.multiple_of(core * share + j * QUAD, QUAD), QUAD)
        mine = terms(j + 8).astype(f32)
        exchange(j).wait_recv()
        summed = mine + incoming(j)[...].astype(f32)
        incoming(j)[...] = (stack[:rows, here].astype(f32) + summed).astype(bf16)
        save(j).start()
        return 0

    lax.fori_loop(0, 8, keep_own, 0)

    def ended(j, _):
        exchange(j).wait_send()
        save(j).wait()
        return 0

    lax.fori_loop(0, 8, ended, 0)
    for by in range(1, SIDE):
        @pl.when(at["y"] + by < SIDE)
        def _():
            for copy in hand_on(by):
                copy.wait_send()
    tail_on.wait_send()
    each(out_rings, ("sent", 0), ("sent", 1), ("sent", 2))


def layer(extents, x, perm, gain, blend, left, weights, out_weight, right, speed, reward, scale):
    rows, width = x.shape
    shard, local_width = weights.shape[1:]
    reqs, inner, pairs = extents.shape[0], left.shape[1], local_width // PAIR
    cuts = [OUT_CUTS[i + 1] - OUT_CUTS[i] for i in range(3)]
    dma = pltpu.SemaphoreType.DMA
    vmem = pl.BlockSpec(memory_space=pltpu.VMEM)
    away = pl.BlockSpec(memory_space=pl.ANY)
    hidden, final, *_ = pl.pallas_call(
        layer_kernel,
        in_specs=[pl.BlockSpec(memory_space=pltpu.SMEM), away] + [vmem] * 10,
        out_specs=[away, vmem, away, away, away],
        out_shape=[
            jax.ShapeDtypeStruct((rows, width // 2), bf16),
            jax.ShapeDtypeStruct((reqs, pairs, PAIR, ATTEND_DIM), f32),
            *(jax.ShapeDtypeStruct((SIDE, SIDE, SIDE, shard, cut), bf16) for cut in cuts),
        ],
        scratch_shapes=[
            pltpu.VMEM((3, SIDE, SIDE, SIDE, shard, local_width), bf16),
            pltpu.VMEM((rows + 16, width), bf16),
            pltpu.VMEM((3, SIDE, rows, width // SIDE), bf16),
            pltpu.VMEM((width // 4, STEP), bf16),
            pltpu.VMEM((rows + 16, STEP), f32),
            pltpu.VMEM((3, rows, local_width), f32),
            pltpu.VMEM((2, rows + 16, PAIR), f32),
            pltpu.VMEM((rows, inner), f32),
            pltpu.VMEM((rows, inner), bf16),
            pltpu.VMEM((reqs, width), bf16),
            pltpu.VMEM((reqs, width), bf16),
            pltpu.VMEM((shard, local_width), bf16),
            pltpu.VMEM((rows, PAIR), f32),
            pltpu.VMEM((CHUNK, QUAD), jnp.int32),
            pltpu.VMEM((reqs, pairs, ATTEND_DIM, PAIR), bf16),
            pltpu.VMEM((reqs, local_width), f32),
            pltpu.VMEM((3, reqs, pairs, ATTEND_DIM, PAIR), bf16),
            pltpu.VMEM((3, reqs, local_width), f32),
            dma, dma((3,)), dma((2,)),
            dma((3, 3, 6)), dma((3, 3, 6)), dma((3, 3, 6)), dma((3, 3, 6)),
            dma((3,)), dma((3,)), dma((3,)), dma((3,)),
            pltpu.SemaphoreType.REGULAR, dma((3, SIDE)), dma((8,)), dma((8,)), dma((8,)),
        ],
        compiler_params=pltpu.CompilerParams(
            collective_id=0, has_side_effects=True, vmem_limit_bytes=61 << 20
        ),
        cost_estimate=pl.CostEstimate(
            flops=100 * 10**9, bytes_accessed=64 << 20, transcendentals=0
        ),
        name="layer",
    )(extents, x, perm, gain, blend, left, weights, out_weight, right, speed, reward, scale)
    return hidden, final


def local(
    incoming_activations,
    standardize_scaling,
    lagged_blending_weights,
    learner_line_permutation,
    learner_acceptor_lookup_slices,
    learner_projection_slices,
    fading_left_matrix,
    fading_right_matrix,
    feature_fading_speed,
    self_reward,
    cluster_scaling_vector,
    prompt_extents,
):
    reqs, span, width = incoming_activations.shape
    rows = reqs * span
    local_width = feature_fading_speed.shape[0]
    x = incoming_activations.reshape(rows, width)
    hidden, final = layer(
        prompt_extents, x, learner_line_permutation.reshape(width // PAIR, PAIR),
        standardize_scaling[None], lagged_blending_weights, fading_left_matrix,
        learner_acceptor_lookup_slices, learner_projection_slices.T, fading_right_matrix,
        feature_fading_speed[None], self_reward[None], cluster_scaling_vector[None],
    )
    stretch_states = final.reshape(reqs, 1, local_width // ATTEND_DIM, ATTEND_DIM * ATTEND_DIM)
    return (hidden.reshape(reqs, span, hidden.shape[1]), stretch_states)


def solution(mesh):
    in_specs = (
        P("req", "seq", None),
        P(),
        P(),
        P(),
        P(None, ("req", "seq"), "tensor"),
        P("tensor", ("req", "seq")),
        P(),
        P(None, "tensor"),
        P("tensor"),
        P("tensor"),
        P("tensor"),
        P("req"),
    )
    out_specs = (P("req", "seq", "tensor"), P("req", "seq", "tensor", None))
    return jax.shard_map(local, mesh=mesh, in_specs=in_specs, out_specs=out_specs, check_vma=False)
```

```python
import functools

import jax
import jax.numpy as jnp
from jax import lax
from jax.experimental import pallas as pl
from jax.experimental.pallas import tpu as pltpu
from jax.sharding import PartitionSpec as P

ATTEND_DIM = 64
PAIR = 128
CHUNK = 128
eps = 1e-05
f32 = jnp.float32
bf16 = jnp.bfloat16
CONTRACT_ROWS = (((0,), (0,)), ((), ()))
CONTRACT_LANES = (((1,), (1,)), ((), ()))


def split_two(value):
    high = value.astype(bf16)
    low = (value - high.astype(f32)).astype(bf16)
    return high, low


def dot32(a, b, dims=(((1,), (0,)), ((), ()))):
    return lax.dot_general(a, b, dims, preferred_element_type=f32)


MESH = pl.DeviceIdType.MESH
ORDERS = (("x", "y", "z"), ("y", "z", "x"), ("z", "x", "y"))
PLACES = (("z", "y", "x"), ("x", "y", "z"), ("y", "x", "z"))
SIDE = 4
STEP = 512
OUT_CUTS = (0, 384, 768, 1024)


def position():
    req = lax.axis_index("req")
    return {"x": req // SIDE, "z": req % SIDE, "y": lax.axis_index("seq")}


def moved(at, axis, by):
    return {**at, axis: (at[axis] + by + SIDE) % SIDE}


def device(at):
    return (lax.axis_index("tensor"), at["x"] * SIDE + at["z"], at["y"])


class Ring:
    def __init__(self, slots, order, places, send, recv, parts):
        self.slots, self.order, self.places = slots, order, places
        self.send, self.recv, self.parts = send, recv, parts
        self.at = position()

    def block(self, phase, where, part):
        index = []
        for axis in self.places:
            turn = self.order.index(axis)
            index.append(slice(None) if turn < phase else where if turn == phase else self.at[axis])
        return self.slots.at[(*index, *part)]

    def copy(self, phase, slot):
        axis = self.order[phase]
        right = slot in (0, 2, 4)
        part = 0 if slot in (0, 3, 4) else 1
        by = 1 if right else -1
        source = self.at if slot < 4 else moved(self.at, axis, -by)
        ref = self.block(phase, source[axis], (self.parts[part],))
        return pltpu.make_async_remote_copy(
            ref, ref, self.send.at[phase, slot], self.recv.at[phase, slot],
            device_id=device(moved(self.at, axis, by)), device_id_type=MESH,
        )

    def start(self, phase):
        for slot in range(4):
            self.copy(phase, slot).start()

    def turn(self, phase):
        for slot in range(2):
            self.copy(phase, slot).wait_recv()
            self.copy(phase, slot + 4).start()

    def near(self, phase):
        for slot in range(2, 4):
            self.copy(phase, slot).wait_recv()

    def far(self, phase):
        for slot in range(4, 6):
            self.copy(phase, slot).wait_recv()

    def settle(self, phase):
        self.near(phase)
        self.far(phase)

    def own_sent(self, phase):
        for slot in range(4):
            self.copy(phase, slot).wait_send()

    def passed_on(self, phase):
        for slot in range(4, 6):
            self.copy(phase, slot).wait_send()

    def sent(self, phase):
        self.own_sent(phase)
        self.passed_on(phase)


def each(rings, *steps):
    for name, phase in steps:
        for ring in rings:
            getattr(ring, name)(phase)


def same_head():
    c = lax.broadcasted_iota(jnp.int32, (PAIR, PAIR), 0) // ATTEND_DIM
    v = lax.broadcasted_iota(jnp.int32, (PAIR, PAIR), 1) // ATTEND_DIM
    return c == v


LEVELS = 7
QUAD = 256


def windows():
    t = lax.broadcasted_iota(jnp.int32, (CHUNK, QUAD), 0)
    s = lax.broadcasted_iota(jnp.int32, (CHUNK, QUAD), 1) % CHUNK
    chosen = [s < t, s > t]
    for level in range(LEVELS):
        middle = (((t >> (level + 1)) << 1) + 1) << level
        late = ((s >= middle) & (s < t)) & (t >= middle)
        early = ((s > t) & (s < middle)) & (t < middle)
        chosen.append(late | early)
    return [jnp.where(c, 1.0, 0.0).astype(bf16) for c in chosen]


def halves(values):
    first_head = lax.broadcasted_iota(jnp.int32, (1, PAIR), 1) < ATTEND_DIM
    return jnp.concatenate(
        [jnp.where(first_head, values, 0.0), jnp.where(first_head, 0.0, values)], axis=0
    ).astype(bf16)


def layer_kernel(
    extents_ref, x_ref, perm_ref, gain_ref, blend_ref, left_ref, w_ref, w_out_ref,
    right_ref, speed_ref, reward_ref, scale_ref,
    out_ref, state_ref, slots0, slots1, slots2,
    slots, stack, mixed, chosen, picked, total, stats, low_rank, lora_ref, last, tail, turned,
    valid_ref, level_of, own_state, own_total, far_state, far_total,
    load_sem, place_sem, tail_sem, send, recv, out_send, out_recv,
    state_send, state_recv, total_send, total_recv, ready, fetch_sem, part_send, part_recv, save_sem,
):
    rows, width = x_ref.shape
    reqs = last.shape[0]
    span = rows // reqs
    at = position()
    half = w_ref.shape[1] // 2
    parts = (slice(0, half), slice(half, 2 * half))
    rings = [
        Ring(slots.at[m], ORDERS[m], PLACES[m], send.at[m], recv.at[m], parts) for m in range(3)
    ]
    load = pltpu.make_async_copy(x_ref, stack.at[pl.ds(0, rows)], load_sem)
    load.start()
    for m in range(3):
        slots[(m, *(at[axis] for axis in PLACES[m]))] = w_ref[m].astype(bf16)
    core = lax.axis_index("tensor")
    partner = (1 - core, lax.axis_index("req"), at["y"])
    far_state[...] = jnp.zeros_like(far_state)
    far_total[...] = jnp.zeros_like(far_total)
    barrier = pltpu.get_barrier_semaphore()
    friends = [device(moved(at, axis, by)) for axis in "xyz" for by in (1, -1)]
    for friend in friends + [device(moved(at, "y", 2)), partner]:
        pl.semaphore_signal(barrier, inc=1, device_id=friend, device_id_type=MESH)
    pl.semaphore_wait(barrier, 8)
    each(rings, ("start", 0))
    load.wait()
    for b in range(reqs):
        end = (b + 1) * span
        last[b : b + 1, :] = stack[end - 16 : end, :].astype(f32)[15:16].astype(bf16)
    tail_on = pltpu.make_async_remote_copy(
        last, tail, tail_sem.at[0], tail_sem.at[1],
        device_id=device(moved(at, "y", 1)), device_id_type=MESH,
    )
    tail_on.start()

    out_slots = (slots0, slots1, slots2)
    out_rings = []
    turned[...] = w_out_ref[...].astype(bf16)
    placed = []
    for i in range(3):
        own = out_slots[i].at[at["x"], at["z"], at["y"]]
        cut = turned.at[:, OUT_CUTS[i] : OUT_CUTS[i + 1]]
        placed.append(pltpu.make_async_copy(cut, own, place_sem.at[i]))
        placed[i].start()
        out_rings.append(
            Ring(out_slots[i], ORDERS[i], ("x", "z", "y"), out_send.at[i], out_recv.at[i], parts)
        )

    table = jnp.concatenate([gain_ref[...], blend_ref[0:3, :]], axis=0)
    first = table.astype(bf16)
    rest = table - first.astype(f32)
    second = rest.astype(bf16)
    third = (rest - second.astype(f32)).astype(bf16)
    each(rings, ("turn", 0))
    tail_on.wait_recv()
    before = jnp.where(at["y"] > 0, tail[...].astype(f32), 0.0).astype(bf16)
    pad = jnp.zeros((16 - reqs - 12, width), bf16)
    stack[rows:, :] = jnp.concatenate([before, first, second, third, pad], axis=0)
    low_rank[...] = jnp.zeros_like(low_rank)

    def row_stats(i, _):
        here = pl.ds(pl.multiple_of(i * 16, 16), 16)
        part = stack[here, :].astype(f32)
        mean = jnp.mean(part, axis=-1, keepdims=True)
        centred = part - mean
        spread = jnp.mean(centred * centred, axis=-1, keepdims=True)
        stats[0, here, :] = jnp.broadcast_to(mean, (16, PAIR))
        stats[1, here, :] = jnp.broadcast_to(lax.rsqrt(spread + eps), (16, PAIR))
        return 0

    lax.fori_loop(0, stack.shape[0] // 16, row_stats, 0)
    each(rings, ("settle", 0), ("start", 1))
    for place in placed:
        place.wait()

    def shifted(values, gain):
        mean, scale = stats[0, :, 0:1], stats[1, :, 0:1]
        row = lax.broadcasted_iota(jnp.int32, (rows, 1), 0)
        normal = (values - mean) * scale * gain
        current = normal[:rows]
        previous = pltpu.roll(current, 1, axis=0)
        for b in range(reqs):
            previous = jnp.where(row == b * span, normal[rows + b : rows + b + 1], previous)
        return current, previous - current

    piece = STEP // 2
    depth = chosen.shape[0]

    def mix_step(step, _):
        here = pl.ds(pl.multiple_of(step * STEP, STEP), STEP)
        y, x0 = step // 2, (step % 2) * 2
        names = []
        for i in range(2):
            for z in range(0, SIDE, 2):
                at_row = (x0 + i) * 8 + z * 2 + y // 2
                low, high = perm_ref[pl.ds(at_row, 1), :], perm_ref[pl.ds(at_row + 2, 1), :]
                low_up, high_up = pltpu.roll(low, 64, axis=1), pltpu.roll(high, 64, axis=1)
                even = y % 2 == 0
                names.append(
                    jnp.where(
                        lax.broadcasted_iota(jnp.int32, (1, 128), 1) < 64,
                        jnp.where(even, low, low_up), jnp.where(even, high_up, high),
                    )
                )
        names = jnp.concatenate(names, axis=1)
        picked[...] = jnp.zeros_like(picked)

        def pick(d, _):
            def one_hot(i, _):
                base = pl.multiple_of(i * 128, 128)
                feature = lax.broadcasted_iota(jnp.int32, (128, STEP), 0) + (base + d * depth)
                chosen[pl.ds(base, 128), :] = (feature == names).astype(f32).astype(bf16)
                return 0

            lax.fori_loop(0, depth // 128, one_hot, 0)
            source = stack[:, pl.ds(pl.multiple_of(d * depth, depth), depth)]
            picked[...] += dot32(source, chosen[...])
            return 0

        lax.fori_loop(0, width // depth, pick, 0)
        for i in range(2):
            values = picked[:, i * piece : (i + 1) * piece]
            own = values[rows + reqs :]
            own = own[0:4] + own[4:8] + own[8:12]
            current, delta = shifted(values, own[0:1])
            blended = [(current + delta * own[1 + j : 2 + j]).astype(bf16) for j in range(3)]
            picked[:rows, i * piece : (i + 1) * piece] = blended[0].astype(f32)
            mixed[1, x0 + i, :, pl.ds(pl.multiple_of(y * piece, piece), piece)] = blended[1]
            mixed[2, y, :, pl.ds(pl.multiple_of((x0 + i) * piece, piece), piece)] = blended[2]
        columns = pl.ds(pl.multiple_of(step * 128, 128), 128)
        for z in range(SIDE):
            pair = [picked[:rows, i * piece + z * 64 : i * piece + (z + 1) * 64] for i in range(2)]
            mixed[0, z, :, columns] = jnp.concatenate(pair, axis=1).astype(bf16)

        current, delta = shifted(stack[:, here].astype(f32), gain_ref[:, here])
        low_rank[...] += dot32(
            (current + delta * blend_ref[3:4, here]).astype(bf16),
            left_ref[pl.ds(pl.multiple_of(step * STEP, STEP), STEP), :],
        )

        for when, group, steps in (
            (0, rings, (("turn", 1),)),
            (2, rings, (("settle", 1), ("start", 2))),
            (3, out_rings, (("start", 0),)),
            (4, out_rings, (("turn", 0),)),
            (5, out_rings, (("settle", 0), ("start", 1))),
            (7, out_rings, (("turn", 1),)),
            (7, rings, (("turn", 2),)),
        ):
            @pl.when(step == when)
            def _():
                each(group, *steps)

        return 0

    lax.fori_loop(0, width // STEP, mix_step, 0)
    lora_ref[...] = jnp.tanh(low_rank[...]).astype(bf16)

    def products(offset, fresh, tiles=(0, 12)):
        def tile(i, _):
            m, n = i // 4, i % 4
            own = jnp.where(m == 0, at["z"], jnp.where(m == 1, at["x"], at["y"]))
            plane = (own + offset) % SIDE
            here = pl.ds(pl.multiple_of(n * 256, 256), 256)
            weight = slots[m, plane, :, :, :, here].reshape(width // SIDE, 256)
            product = dot32(mixed[m, plane], weight)
            if fresh:
                total[m, :, here] = product
            elif offset == 2:
                mixed[m, own, :, here] = (total[m, :, here] + product).astype(bf16)
            else:
                total[m, :, here] += product
            return 0

        lax.fori_loop(*tiles, tile, 0)

    products(0, True)
    each(rings, ("near", 2))
    products(1, False)
    products(3, False)
    each(out_rings, ("settle", 1))
    sums = [(slice(CHUNK * i, CHUNK * (i + 1)), slice(0, QUAD)) for i in range(8)]
    sums.append((slice(0, CHUNK), slice(QUAD, 2 * QUAD)))
    row = lax.broadcasted_iota(jnp.int32, (rows, PAIR), 0)
    token = at["y"] * span + row % span
    inside = jnp.zeros((rows, PAIR), f32)
    for b in range(reqs):
        inside = jnp.where((row // span == b) & (token < extents_ref[b]), 1.0, inside)
    valid_ref[...] = inside

    for i, window in enumerate(windows()):
        chosen[sums[i]] = window
    t = lax.broadcasted_iota(jnp.int32, (CHUNK, QUAD), 0)
    s = lax.broadcasted_iota(jnp.int32, (CHUNK, QUAD), 1) % CHUNK
    level = jnp.full((CHUNK, QUAD), LEVELS, jnp.int32)
    for i in range(LEVELS):
        level = jnp.where(((t >> i) == (s >> i) + 1) & (((t >> i) & 1) == 1), i, level)
    level_of[...] = level
    local_width = total.shape[2]

    def place(m, offset):
        return mixed.at[m, (at[PLACES[m][0]] + offset) % SIDE]

    high_decay, low_decay = place(1, 3), place(2, 3)

    def decay(q, _):
        lanes = pl.ds(pl.multiple_of(q * QUAD, QUAD), QUAD)
        rate = jnp.exp(dot32(lora_ref[...], right_ref[:, lanes]))
        high, low = split_two(-speed_ref[:, lanes] * rate * valid_ref[:, 0:1])
        high_decay[:, lanes], low_decay[:, lanes] = high, low
        return 0

    lax.fori_loop(0, local_width // QUAD, decay, 0)

    def split_decay(rows_c, lanes):
        return jnp.concatenate([high_decay[rows_c, lanes], low_decay[rows_c, lanes]], axis=0)

    each(rings, ("sent", 0), ("sent", 1), ("own_sent", 2))

    def level_decay(n, c, lanes):
        m, part = (n - 1) // 2, (n - 1) % 2
        return (
            m, at[PLACES[m][0]], 2 * part + c // 2, pl.ds(c % 2 * 2, 2), slice(None), lanes
        )

    def fade(i, _):
        q, c = i // 4, i % 4
        lanes = pl.ds(pl.multiple_of(q * QUAD, QUAD), QUAD)
        both = split_decay(pl.ds(pl.multiple_of(c * CHUNK, CHUNK), CHUNK), lanes)
        for n in range(1, LEVELS):
            faint = jnp.exp(dot32(chosen[sums[2 + n]], both)).astype(bf16)
            slots[level_decay(n, c, lanes)] = faint.reshape(2, CHUNK // 2, QUAD)
        return 0

    lax.fori_loop(0, local_width // QUAD * (rows // CHUNK), fade, 0)
    each(out_rings, ("start", 2))
    for m in range(3):
        rings[m].far(2)
        products(2, False, (4 * m, 4 * m + 4))
    pl.semaphore_signal(ready, inc=1, device_id=partner, device_id_type=MESH)
    rkv = [place(m, 0) for m in range(3)]
    faded, normed = place(0, 1), place(0, 3)
    y_buf = total.at[0]
    share = width // 2

    def tiles(m, offsets):
        planes = [(at[PLACES[m][0]] + offset) % SIDE for offset in offsets]

        def tile(j):
            plane = jnp.where(j < 4, planes[0], planes[1])
            return mixed.at[m, plane, :, pl.ds(pl.multiple_of(j % 4 * QUAD, QUAD), QUAD)]

        return tile

    outgoing, incoming = tiles(1, (1, 2)), tiles(2, (1, 2))
    keep = same_head()
    ones = jnp.where(keep, 1.0, 0.0).astype(bf16)
    head_sum = jnp.concatenate([ones, ones], axis=0)
    first_head = lax.broadcasted_iota(jnp.int32, (1, PAIR), 1) < ATTEND_DIM

    def over_head(values):
        return dot32(jnp.concatenate(split_two(values), axis=1), head_sum)

    def prepare(q, _):
        lanes = pl.ds(pl.multiple_of(q * QUAD, QUAD), QUAD)
        valid = valid_ref[:, 0:1]
        for b in range(reqs):
            before, after, total = [], [], []
            for c in range(span // CHUNK):
                rows_c = slice(b * span + c * CHUNK, b * span + (c + 1) * CHUNK)
                both = split_decay(rows_c, lanes)
                w = both[:CHUNK].astype(f32) + both[CHUNK:].astype(f32)
                before.append(dot32(chosen[sums[0]], both))
                after.append(dot32(chosen[sums[1]], both))
                total.append(before[c][CHUNK - 1 :] + w[CHUNK - 1 :])
            own_total[b : b + 1, lanes] = total[0] + total[1]
            at0 = slice(b * span, b * span + CHUNK)
            at1 = slice(b * span + CHUNK, (b + 1) * span)
            whole = slice(b * span, (b + 1) * span)
            r0, r1 = rkv[0][at0, lanes].astype(f32), rkv[0][at1, lanes].astype(f32)
            k0 = rkv[1][at0, lanes].astype(f32) * valid[at0]
            k1 = rkv[1][at1, lanes].astype(f32) * valid[at1]
            faded[at0, lanes] = (r0 * jnp.exp(before[0])).astype(bf16)
            faded[at1, lanes] = (r1 * jnp.exp(before[1] + total[0])).astype(bf16)
            query1 = (r1 * jnp.exp(before[1])).astype(bf16)
            key0 = (k0 * jnp.exp(after[0])).astype(bf16)
            keys = jnp.concatenate(
                [(k0 * jnp.exp(after[0] + total[1])).astype(bf16), (k1 * jnp.exp(after[1])).astype(bf16)],
                axis=0,
            )
            value = rkv[2][whole, lanes]
            bonus0 = r0 * k0 * reward_ref[:, lanes]
            bonus1 = r1 * k1 * reward_ref[:, lanes]
            for p in range(2):
                pair = slice(p * PAIR, (p + 1) * PAIR)
                here = pl.ds(pl.multiple_of(q * QUAD + p * PAIR, PAIR), PAIR)
                grown = dot32(value[:, pair], keys[:, pair], CONTRACT_ROWS)
                own_state[b, 2 * q + p] = jnp.where(
                    first_head, grown[:ATTEND_DIM], grown[ATTEND_DIM:]
                ).astype(bf16)
                grown0 = dot32(value[:CHUNK, pair], key0[:, pair], CONTRACT_ROWS)
                grown0 = jnp.where(keep, grown0, 0.0).astype(bf16)
                y_buf[at0, here] = over_head(bonus0[:, pair]) * value[:CHUNK, pair].astype(f32)
                y_buf[at1, here] = over_head(bonus1[:, pair]) * value[CHUNK:, pair].astype(
                    f32
                ) + dot32(query1[:, pair], grown0, CONTRACT_LANES)

        return 0

    lax.fori_loop(0, local_width // QUAD, prepare, 0)

    def hand_on(by):
        to = device(moved(at, "y", by))
        return [
            pltpu.make_async_remote_copy(
                own, far.at[by - 1], s_sem.at[by - 1], r_sem.at[by - 1],
                device_id=to, device_id_type=MESH,
            )
            for own, far, s_sem, r_sem in (
                (own_state, far_state, state_send, state_recv),
                (own_total, far_total, total_send, total_recv),
            )
        ]

    for by in range(1, SIDE):
        @pl.when(at["y"] + by < SIDE)
        def _():
            for copy in hand_on(by):
                copy.start()

    def within(i, _):
        q, c = i // 4, i % 4
        rows_c = pl.ds(pl.multiple_of(c * CHUNK, CHUNK), CHUNK)
        row = lax.broadcasted_iota(jnp.int32, (CHUNK, 1), 0)
        valid = valid_ref[rows_c, 0:1]
        for p in range(2):
            pair = slice(p * PAIR, (p + 1) * PAIR)
            here = pl.ds(pl.multiple_of(q * QUAD + p * PAIR, PAIR), PAIR)
            r = rkv[0][rows_c, here].astype(f32)
            k = rkv[1][rows_c, here].astype(f32) * valid
            scores = jnp.zeros((CHUNK, QUAD), f32)
            for n in range(LEVELS):
                side = jnp.where(((row >> n) & 1) == 1, r, k)
                if n > 0:
                    side = side * slots[level_decay(n, c, here)].reshape(CHUNK, PAIR).astype(f32)
                found = dot32(side.astype(bf16), halves(side), CONTRACT_LANES)
                scores = jnp.where(level_of[...] == n, found, scores)
            values = halves(rkv[2][rows_c, here].astype(f32))
            y_buf[rows_c, here] += dot32(scores.astype(bf16), values)

        @pl.when(i == 3)
        def _():
            each(out_rings, ("turn", 2))

        return 0

    lax.fori_loop(0, local_width // QUAD * (rows // CHUNK), within, 0)

    def fetch(i, offset):
        axis = ORDERS[i][2]
        index = [slice(None)] * 3
        index["xzy".index(axis)] = (at[axis] + offset) % SIDE
        cut = slice(OUT_CUTS[i], OUT_CUTS[i + 1])
        return pltpu.make_async_copy(
            out_slots[i].at[tuple(index)], slots.at[(0, *index, slice(None), cut)],
            fetch_sem.at[i, offset],
        )

    each(rings, ("passed_on", 2))
    each(out_rings, ("near", 2))
    for i in range(3):
        for offset in (0, 1, 3):
            fetch(i, offset).start()
    for by in range(1, SIDE):
        @pl.when(at["y"] >= by)
        def _():
            for copy in hand_on(by):
                copy.wait_recv()

    def finish(p, _):
        here = pl.ds(pl.multiple_of(p * PAIR, PAIR), PAIR)
        for b in range(reqs):
            whole = slice(b * span, (b + 1) * span)
            near = far_total[0, b : b + 1, here]
            state = (
                far_state[0, b, p].astype(f32)
                + jnp.exp(near) * far_state[1, b, p].astype(f32)
                + jnp.exp(near + far_total[1, b : b + 1, here]) * far_state[2, b, p].astype(f32)
            )
            final = jnp.exp(own_total[b : b + 1, here]) * state + own_state[b, p].astype(f32)
            state_ref[b, p] = final.T
            y = y_buf[whole, here] + dot32(faded[whole, here], halves(state), CONTRACT_LANES)
            centred = y - over_head(y) * (1.0 / ATTEND_DIM)
            spread = over_head(centred * centred) * (1.0 / ATTEND_DIM)
            scaled = centred * lax.rsqrt(spread + eps) * scale_ref[:, here]
            normed[whole, here] = (scaled * valid_ref[whole, 0:1]).astype(bf16)
        return 0

    lax.fori_loop(0, local_width // PAIR, finish, 0)
    each(out_rings, ("far", 2))
    for i in range(3):
        fetch(i, 2).start()
    for i in range(3):
        for offset in range(SIDE):
            fetch(i, offset).wait()

    def terms(t):
        weight = slots[0, 2 * jnp.where(t < 8, 1 - core, core) + t % 8 // SIDE, t % SIDE]
        weight = weight.reshape(QUAD, local_width)
        return dot32(normed[...], weight, CONTRACT_LANES).astype(bf16)

    def exchange(j):
        return pltpu.make_async_remote_copy(
            outgoing(j), incoming(j), part_send.at[j], part_recv.at[j],
            device_id=partner, device_id_type=MESH,
        )

    pl.semaphore_wait(ready, 1)

    def give(j, _):
        outgoing(j)[...] = terms(j)
        exchange(j).start()
        return 0

    lax.fori_loop(0, 8, give, 0)

    def save(j):
        here = pl.ds(pl.multiple_of(j * QUAD, QUAD), QUAD)
        return pltpu.make_async_copy(incoming(j), out_ref.at[:, here], save_sem.at[j])

    def keep_own(j, _):
        here = pl.ds(pl.multiple_of(core * share + j * QUAD, QUAD), QUAD)
        mine = terms(j + 8).astype(f32)
        exchange(j).wait_recv()
        summed = mine + incoming(j)[...].astype(f32)
        incoming(j)[...] = (stack[:rows, here].astype(f32) + summed).astype(bf16)
        save(j).start()
        return 0

    lax.fori_loop(0, 8, keep_own, 0)

    def ended(j, _):
        exchange(j).wait_send()
        save(j).wait()
        return 0

    lax.fori_loop(0, 8, ended, 0)
    for by in range(1, SIDE):
        @pl.when(at["y"] + by < SIDE)
        def _():
            for copy in hand_on(by):
                copy.wait_send()
    tail_on.wait_send()
    each(out_rings, ("sent", 0), ("sent", 1), ("sent", 2))


def layer(extents, x, perm, gain, blend, left, weights, out_weight, right, speed, reward, scale):
    rows, width = x.shape
    shard, local_width = weights.shape[1:]
    reqs, inner, pairs = extents.shape[0], left.shape[1], local_width // PAIR
    cuts = [OUT_CUTS[i + 1] - OUT_CUTS[i] for i in range(3)]
    dma = pltpu.SemaphoreType.DMA
    vmem = pl.BlockSpec(memory_space=pltpu.VMEM)
    away = pl.BlockSpec(memory_space=pl.ANY)
    hidden, final, *_ = pl.pallas_call(
        layer_kernel,
        in_specs=[pl.BlockSpec(memory_space=pltpu.SMEM), away] + [vmem] * 10,
        out_specs=[away, vmem, away, away, away],
        out_shape=[
            jax.ShapeDtypeStruct((rows, width // 2), bf16),
            jax.ShapeDtypeStruct((reqs, pairs, PAIR, ATTEND_DIM), f32),
            *(jax.ShapeDtypeStruct((SIDE, SIDE, SIDE, shard, cut), bf16) for cut in cuts),
        ],
        scratch_shapes=[
            pltpu.VMEM((3, SIDE, SIDE, SIDE, shard, local_width), bf16),
            pltpu.VMEM((rows + 16, width), bf16),
            pltpu.VMEM((3, SIDE, rows, width // SIDE), bf16),
            pltpu.VMEM((width // 4, STEP), bf16),
            pltpu.VMEM((rows + 16, STEP), f32),
            pltpu.VMEM((3, rows, local_width), f32),
            pltpu.VMEM((2, rows + 16, PAIR), f32),
            pltpu.VMEM((rows, inner), f32),
            pltpu.VMEM((rows, inner), bf16),
            pltpu.VMEM((reqs, width), bf16),
            pltpu.VMEM((reqs, width), bf16),
            pltpu.VMEM((shard, local_width), bf16),
            pltpu.VMEM((rows, PAIR), f32),
            pltpu.VMEM((CHUNK, QUAD), jnp.int32),
            pltpu.VMEM((reqs, pairs, ATTEND_DIM, PAIR), bf16),
            pltpu.VMEM((reqs, local_width), f32),
            pltpu.VMEM((3, reqs, pairs, ATTEND_DIM, PAIR), bf16),
            pltpu.VMEM((3, reqs, local_width), f32),
            dma, dma((3,)), dma((2,)),
            dma((3, 3, 6)), dma((3, 3, 6)), dma((3, 3, 6)), dma((3, 3, 6)),
            dma((3,)), dma((3,)), dma((3,)), dma((3,)),
            pltpu.SemaphoreType.REGULAR, dma((3, SIDE)), dma((8,)), dma((8,)), dma((8,)),
        ],
        compiler_params=pltpu.CompilerParams(
            collective_id=0, has_side_effects=True, vmem_limit_bytes=61 << 20
        ),
        cost_estimate=pl.CostEstimate(
            flops=100 * 10**9, bytes_accessed=64 << 20, transcendentals=0
        ),
        name="layer",
    )(extents, x, perm, gain, blend, left, weights, out_weight, right, speed, reward, scale)
    return hidden, final


def local(
    incoming_activations,
    standardize_scaling,
    lagged_blending_weights,
    learner_line_permutation,
    learner_acceptor_lookup_slices,
    learner_projection_slices,
    fading_left_matrix,
    fading_right_matrix,
    feature_fading_speed,
    self_reward,
    cluster_scaling_vector,
    prompt_extents,
):
    reqs, span, width = incoming_activations.shape
    rows = reqs * span
    local_width = feature_fading_speed.shape[0]
    x = incoming_activations.reshape(rows, width)
    hidden, final = layer(
        prompt_extents, x, learner_line_permutation.reshape(width // PAIR, PAIR),
        standardize_scaling[None], lagged_blending_weights, fading_left_matrix,
        learner_acceptor_lookup_slices, learner_projection_slices.T, fading_right_matrix,
        feature_fading_speed[None], self_reward[None], cluster_scaling_vector[None],
    )
    stretch_states = final.reshape(reqs, 1, local_width // ATTEND_DIM, ATTEND_DIM * ATTEND_DIM)
    return (hidden.reshape(reqs, span, hidden.shape[1]), stretch_states)


def solution(mesh):
    in_specs = (
        P("req", "seq", None),
        P(),
        P(),
        P(),
        P(None, ("req", "seq"), "tensor"),
        P("tensor", ("req", "seq")),
        P(),
        P(None, "tensor"),
        P("tensor"),
        P("tensor"),
        P("tensor"),
        P("req"),
    )
    out_specs = (P("req", "seq", "tensor"), P("req", "seq", "tensor", None))
    return jax.shard_map(local, mesh=mesh, in_specs=in_specs, out_specs=out_specs, check_vma=False)
```
